32 devices in a mesh: row: 4 (over x, core), col: 8 (over z, y).
Axes of the slice: x: 2, y: 2, z: 4, core: 2. Of those that a mesh axis runs over, the one named last changes fastest.
Arguments:
- vectors: bfloat16 [1, 16, 4096], P(None, None, ('col', 'row')), may hold values from -110 to 110
- h_tiles: bfloat16 [1, 4, 256, 128, 128], P(None, 'row', 'col'), may hold values from -0.15625 to 0.15625
- h_list: int32 [1, 4, 256], P(None, 'row', 'col'), may hold values from -1 to 31, as said below
- j_tiles: bfloat16 [1, 4, 96, 128, 128], P(None, 'row', 'col'), may hold values from -0.25 to 0.25
- j_list: int32 [1, 4, 96], P(None, 'row', 'col'), may hold values from -1 to 63, as said below
Outputs:
- basis: float32 [1, 16, 4096], P(None, None, ('row', 'col'))
- transitions: float32 [1, 2, 16, 16], replicated
The draws below stay inside these ranges and needn't reach their ends.
Inputs may be any that keep to these rules, and one draw needn't show every extreme that they name: `h_list`: each block's 32 entries list distinct tile positions first and then -1; at most 32 positions a block, and some block lists all 32. `j_list`: each block's 12 entries list distinct codes first and then -1; at most 12 codes a block, and some block lists all 12.
All inputs are finite; a program needn't handle non-finite values.
Results may differ from the reference program's by a relative error of at most 0.0003.
Values may be sent and summed in bfloat16 or wider, within the bound.
No kernel may reach another device: no remote copies, remote signals or barrier semaphores. Data moves between devices by JAX's collectives and lax.ppermute only.
A program may use at most 64 MiB of HBM per device.

```python
import math
import jax
import jax.numpy as jnp
from jax import lax

K = 16
TILE = 128
RT = 8
SECT = 1
HSLOT = 32
JSLOT = 12
NSIT = 6
NS = 4096
CT = 4
N_ROW = 4
N_COL = 8


def listed_codes(key, slot_count, position_count):
    block_count = SECT * N_ROW * N_COL
    key_order, key_count, key_full, key_pick = jax.random.split(key, 4)
    orders = jax.vmap(lambda single: jax.random.permutation(single, position_count))(jax.random.split(key_order, block_count))
    sparse_count = jax.random.randint(key_count, (block_count,), slot_count // 4, slot_count // 2 + 1)
    filled = jax.random.randint(key_full, (block_count,), 0, 8) == 0
    chosen = jax.random.randint(key_pick, (), 0, block_count)
    counts = jnp.where(filled | (jnp.arange(block_count) == chosen), slot_count, sparse_count)
    codes = jnp.where(jnp.arange(slot_count)[None, :] < counts[:, None], orders[:, :slot_count], -1)
    return codes.reshape(SECT, N_ROW, N_COL * slot_count).astype(jnp.int32)


def draw_h_list(key, part):
    return listed_codes(jax.random.fold_in(key, 11), HSLOT, RT * CT)


def draw_j_list(key, part):
    return listed_codes(jax.random.fold_in(key, 23), JSLOT, 2 * RT * CT)


def draw_vectors(key, part):
    key_noise, key_common, key_scale = jax.random.split(jax.random.fold_in(key, 37), 3)
    noise_part = jnp.clip(jax.random.normal(key_noise, (SECT, K, NS), jnp.float32), -4.0, 4.0)
    common = jnp.clip(jax.random.normal(key_common, (SECT, 1, NS), jnp.float32), -4.0, 4.0)
    mixing = 0.7
    spread = math.log(10.0)
    column_scale = jnp.exp(jax.random.uniform(key_scale, (SECT, K, 1), jnp.float32) * spread)
    row_scale = 0.5 + jnp.arange(NS, dtype=jnp.float32) / NS
    return (column_scale * row_scale * (noise_part + mixing * common)).astype(jnp.bfloat16)


def shard_levels(stream_key, dims, pieces, smallest, largest):
    level, own = 1.0, jax.random.fold_in(stream_key, 6)
    for axis_at, shards_of in pieces:
        draws = jnp.exp(jax.random.uniform(jax.random.fold_in(own, axis_at), (shards_of,), jnp.float32, smallest / len(pieces), largest / len(pieces)))
        level = level * jnp.repeat(draws, dims[axis_at] // shards_of).reshape([-1 if axis == axis_at else 1 for axis in range(len(dims))])
    return level


def gaussian(own_key, shape, width, reach, shards=(), held_as=jnp.bfloat16):
    gain = shard_levels(own_key, shape, shards, -0.22, 0.18) if shards else 1.0
    entries = jax.random.normal(own_key, shape, jnp.float32) * width * gain
    return jnp.minimum(jnp.maximum(entries, -reach), reach).astype(held_as)


def setup_inputs(seed: int = 0) -> dict:
    arg_keys = jax.random.split(jax.random.key(seed), 6)
    vectors = draw_vectors(jax.random.fold_in(arg_keys[5], 71), 0)
    h_tiles = gaussian(arg_keys[1], (SECT, N_ROW, N_COL * HSLOT, TILE, TILE), (NS // 3) ** -0.5, 0.15625, ((1, 4), (2, 8)))
    h_list = draw_h_list(jax.random.fold_in(arg_keys[5], 71), 0)
    j_tiles = gaussian(arg_keys[3], (SECT, N_ROW, N_COL * JSLOT, TILE, TILE), (NS // 8) ** -0.5, 0.25, ((1, 4), (2, 8)))
    j_list = draw_j_list(jax.random.fold_in(arg_keys[5], 71), 0)
    return {"vectors": vectors, "h_tiles": h_tiles, "h_list": h_list, "j_tiles": j_tiles, "j_list": j_list}


exact_precision = lax.Precision.HIGHEST

def tile_products(tile_data, code_data, vector_set, operator_count):
    slot_count = code_data.shape[1] // N_COL
    position_count = RT * CT
    column_vectors = vector_set.reshape(K, N_COL, CT, TILE).astype(jnp.float32)

    def one_row(inputs):
        tile_row, code_row = inputs
        tile_row = tile_row.reshape(N_COL, slot_count, TILE, TILE).astype(jnp.float32)
        code_row = code_row.reshape(N_COL, slot_count)
        places = code_row % position_count
        operator = code_row // position_count
        column_hot = (places[:, :, None] % CT == jnp.arange(CT)[None, None, :]).astype(jnp.float32)
        picked = jnp.einsum('jqc,kjcb->jqkb', column_hot, column_vectors, precision=exact_precision)
        product = jnp.einsum('jqab,jqkb->jqka', tile_row, picked, precision=exact_precision)
        row_hot = ((operator[:, :, None, None] == jnp.arange(operator_count)[None, None, :, None]) & (places[:, :, None, None] // CT == jnp.arange(RT)[None, None, None, :]) & (code_row[:, :, None, None] >= 0)).astype(jnp.float32)
        result = jnp.einsum('jqor,jqka->okra', row_hot, product, precision=exact_precision)
        return result.reshape(operator_count, K, RT * TILE)
    stacked = lax.map(one_row, (tile_data, code_data))
    return stacked.transpose(1, 2, 0, 3).reshape(operator_count, K, NS)

def orthonormal_root(gram):
    scale = jnp.sqrt(jnp.sum(gram * gram) + 1e-06)
    iterate = gram / scale
    identity = jnp.eye(K, dtype=jnp.float32)
    inverse_root = identity
    for iteration in range(NSIT):
        middle = 1.5 * identity - 0.5 * jnp.dot(inverse_root, iterate, precision=exact_precision)
        iterate = jnp.dot(iterate, middle, precision=exact_precision)
        inverse_root = jnp.dot(middle, inverse_root, precision=exact_precision)
    return (inverse_root, scale)

def reference(vectors, h_tiles, h_list, j_tiles, j_list):
    basis_list = []
    transition_list = []
    for sector in range(SECT):
        projected = tile_products(h_tiles[sector], h_list[sector], vectors[sector], 1)[0]
        applied = tile_products(j_tiles[sector], j_list[sector], vectors[sector], 2)
        gram = jnp.einsum('kp,lp->kl', projected, projected, precision=exact_precision)
        inverse_root, scale = orthonormal_root(gram)
        basis = jnp.sqrt(NS / scale) * jnp.einsum('mk,mp->kp', inverse_root, projected, precision=exact_precision)
        elements = jnp.einsum('kp,alp->akl', basis, applied, precision=exact_precision) / math.sqrt(NS)
        basis_list.append(basis)
        transition_list.append(elements)
    return (jnp.stack(basis_list), jnp.stack(transition_list))
```

```python
import functools
import math

import jax
import jax.numpy as jnp
from jax import lax
from jax.experimental import pallas as pl
from jax.experimental.pallas import tpu as pltpu
from jax.sharding import PartitionSpec as P

NSIT = 6
J_OPERATORS = 2

exact_precision = lax.Precision.HIGHEST


def digits_of(size):
    digits, stride = [], 1
    while stride < size:
        rest = size // stride
        factor = next(f for f in range(2, rest + 1) if rest % f == 0)
        digits.append((stride, factor))
        stride *= factor
    return digits


def moved(index, digit, shift):
    stride, factor = digit
    value = index // stride % factor
    return index + ((value + shift) % factor - value) * stride


def sent(x, axis, digit, shift):
    size = lax.axis_size(axis)
    return lax.ppermute(x, axis, [(i, moved(i, digit, shift)) for i in range(size)])


def summed(x, axis, digit):
    parts = [sent(x, axis, digit, shift) for shift in range(1, digit[1])]
    return functools.reduce(jnp.add, parts, x)


def scatter_digit(size, piece, tile):
    for stride, factor in digits_of(size):
        if factor == 2 and piece * stride % tile == 0:
            return (stride, factor)
    return None


def product_kernel(layout, place_ref, h_list_ref, j_list_ref, vector_ref, h_ref, j_ref, *refs):
    column_tiles, row_tiles, group, halves = layout
    outs, total = refs[:halves], refs[halves]
    kept_tiles = row_tiles // halves
    vectors, tile = vector_ref.shape[1], h_ref.shape[-1]
    total[...] = jnp.zeros_like(total)
    place = place_ref[0]
    for s in range(vector_ref.shape[0]):
        for tiles, codes in ((h_ref, h_list_ref), (j_ref, j_list_ref)):
            slots = tiles.shape[1]
            for q in range(slots):
                code = codes[s * slots + q]
                spot = jnp.maximum(code, 0)
                strip = spot // column_tiles
                column = spot - strip * column_tiles
                operator = strip // row_tiles
                row = strip - operator * row_tiles
                if tiles is j_ref:
                    operator = operator + 1
                half = row // group % halves
                local = row // (group * halves) * group + row % group
                half = jnp.where(half == place, 0, 1) if halves > 1 else 0
                at = (half * kept_tiles + local) * (J_OPERATORS + 1) + operator
                at = jnp.where(code >= 0, at, row_tiles * (J_OPERATORS + 1))
                picked = vector_ref[s, :, pl.ds(pl.multiple_of(column * tile, tile), tile)]
                product = lax.dot_general(
                    picked, tiles[s, q], (((1,), (1,)), ((), ())), preferred_element_type=jnp.float32
                )
                total[s, at] += product
    count = kept_tiles * (J_OPERATORS + 1)
    for half, out in enumerate(outs):
        out[...] = total[:, half * count : (half + 1) * count]


def tile_products(place, h_list, j_list, vector_block, h_tiles, j_tiles, layout):
    column_tiles, row_tiles, group, halves = layout
    sectors, vectors = vector_block.shape[:2]
    tile = h_tiles.shape[-1]
    count = row_tiles // halves * (J_OPERATORS + 1)
    smem = pl.BlockSpec(memory_space=pltpu.SMEM)
    vmem = pl.BlockSpec(memory_space=pltpu.VMEM)
    shape = jax.ShapeDtypeStruct((sectors, count, vectors, tile), jnp.float32)
    return pl.pallas_call(
        functools.partial(product_kernel, layout),
        out_shape=[shape] * halves,
        in_specs=[smem, smem, smem, vmem, vmem, vmem],
        out_specs=[vmem] * halves,
        scratch_shapes=[
            pltpu.VMEM((sectors, row_tiles * (J_OPERATORS + 1) + 1, vectors, tile), jnp.float32)
        ],
        compiler_params=pltpu.CompilerParams(vmem_limit_bytes=8 << 20),
        name="tile_products",
    )(place, h_list, j_list, vector_block, h_tiles, j_tiles)


def gram_kernel(x_ref, out_ref):
    sectors, count = x_ref.shape[:2]
    operators = J_OPERATORS + 1
    for s in range(sectors):
        for o in range(operators):
            part = None
            for t in range(count // operators):
                term = lax.dot_general(
                    x_ref[s, t * operators],
                    x_ref[s, t * operators + o],
                    (((1,), (1,)), ((), ())),
                    precision=exact_precision,
                    preferred_element_type=jnp.float32,
                )
                part = term if part is None else part + term
            out_ref[s, o] = part


def gram_parts(x):
    sectors, _, vectors, _ = x.shape
    vmem = pl.BlockSpec(memory_space=pltpu.VMEM)
    return pl.pallas_call(
        gram_kernel,
        out_shape=jax.ShapeDtypeStruct((sectors, J_OPERATORS + 1, vectors, vectors), jnp.float32),
        in_specs=[vmem],
        out_specs=vmem,
        compiler_params=pltpu.CompilerParams(vmem_limit_bytes=4 << 20),
        name="gram_parts",
    )(x)


def root_kernel(layout, own_ref, gram_ref, x_ref, basis_ref, elements_ref):
    total_rows, own_tiles = layout
    vectors, tile = x_ref.shape[2:]
    operators = J_OPERATORS + 1

    def dot(a, b):
        return jnp.dot(a, b, precision=exact_precision, preferred_element_type=jnp.float32)

    rows = lax.broadcasted_iota(jnp.int32, (vectors, vectors), 0)
    columns = lax.broadcasted_iota(jnp.int32, (vectors, vectors), 1)
    identity = jnp.where(rows == columns, 1.0, 0.0).astype(jnp.float32)
    for s in range(x_ref.shape[0]):
        gram = gram_ref[s, 0]
        squares = jnp.sum(jnp.sum(gram * gram, axis=1, keepdims=True), axis=0, keepdims=True)
        scale = jnp.sqrt(squares + 1e-06)
        iterate = gram / scale
        root = None
        for iteration in range(NSIT):
            product = iterate if root is None else dot(root, iterate)
            middle = 1.5 * identity - 0.5 * product
            root = middle if root is None else dot(middle, root)
            if iteration < NSIT - 1:
                iterate = dot(iterate, middle)
        factor = jnp.sqrt(total_rows / scale)
        turned = root.T * factor
        for t in range(own_tiles):
            at = (own_ref[0] + t) * operators
            basis_ref[s, :, t * tile : (t + 1) * tile] = dot(turned, x_ref[s, at])
        for a in range(J_OPERATORS):
            elements_ref[s, a] = dot(turned, gram_ref[s, a + 1]) / math.sqrt(total_rows)


def orthonormal(own, gram, x, total_rows, own_tiles):
    sectors, _, vectors, tile = x.shape
    smem = pl.BlockSpec(memory_space=pltpu.SMEM)
    vmem = pl.BlockSpec(memory_space=pltpu.VMEM)
    return pl.pallas_call(
        functools.partial(root_kernel, (total_rows, own_tiles)),
        out_shape=[
            jax.ShapeDtypeStruct((sectors, vectors, own_tiles * tile), jnp.float32),
            jax.ShapeDtypeStruct((sectors, J_OPERATORS, vectors, vectors), jnp.float32),
        ],
        in_specs=[smem, vmem, vmem],
        out_specs=[vmem, vmem],
        compiler_params=pltpu.CompilerParams(vmem_limit_bytes=4 << 20),
        name="orthonormal",
    )(own, gram, x)


def per_device(vectors, h_tiles, h_list, j_tiles, j_list):
    sectors, _, piece = vectors.shape
    tile = h_tiles.shape[-1]
    n_row, n_col = lax.axis_size("row"), lax.axis_size("col")
    column = lax.axis_index("col")
    block_rows = piece * n_col
    row_tiles = block_rows // tile
    column_tiles = piece * n_row // tile
    total_rows = block_rows * n_row
    digit = scatter_digit(n_col, piece, tile)
    halves = 1 if digit is None else 2
    group = 1 if digit is None else piece * digit[0] // tile
    layout = (column_tiles, row_tiles, group, halves)
    place = jnp.zeros((1,), jnp.int32)
    if digit is not None:
        place = place + column // digit[0] % 2

    vector_block = lax.all_gather(vectors, "row", axis=2, tiled=True)
    outs = tile_products(
        place,
        h_list.reshape(-1),
        j_list.reshape(-1),
        vector_block,
        h_tiles.reshape(sectors, -1, tile, tile),
        j_tiles.reshape(sectors, -1, tile, tile),
        layout,
    )
    x = outs[0]
    if digit is not None:
        x = x + sent(outs[1], "col", digit, 1)
    for other in digits_of(n_col):
        if other != digit:
            x = summed(x, "col", other)

    gram = gram_parts(x)
    for other in digits_of(n_row):
        gram = summed(gram, "row", other)
    if digit is not None:
        gram = summed(gram, "col", digit)

    own_tiles = max(1, piece // tile)
    first = column * piece // tile
    own = first if digit is None else first // (group * 2) * group + first % group
    basis, elements = orthonormal(own.reshape(1).astype(jnp.int32), gram, x, total_rows, own_tiles)
    if piece < tile:
        basis = lax.dynamic_slice_in_dim(basis, column * piece % tile, piece, 2)
    return (basis, elements)


def solution(mesh):
    return jax.shard_map(
        per_device,
        mesh=mesh,
        in_specs=(
            P(None, None, ("col", "row")),
            P(None, "row", "col", None, None),
            P(None, "row", "col"),
            P(None, "row", "col", None, None),
            P(None, "row", "col"),
        ),
        out_specs=(P(None, None, ("row", "col")), P()),
        check_vma=False,
    )
```

```python
import functools
import math

import jax
import jax.numpy as jnp
from jax import lax
from jax.experimental import pallas as pl
from jax.experimental.pallas import tpu as pltpu
from jax.sharding import PartitionSpec as P

NSIT = 6
J_OPERATORS = 2
LANES = 128

exact_precision = lax.Precision.HIGHEST


def digits_of(size):
    digits, stride = [], 1
    while stride < size:
        rest = size // stride
        factor = next(f for f in range(2, rest + 1) if rest % f == 0)
        digits.append((stride, factor))
        stride *= factor
    return digits


def moved(index, digit, shift):
    stride, factor = digit
    value = index // stride % factor
    return index + ((value + shift) % factor - value) * stride


def sent(x, axis, digit, shift):
    size = lax.axis_size(axis)
    return lax.ppermute(x, axis, [(i, moved(i, digit, shift)) for i in range(size)])


def across(x, row_mask, column_mask):
    n_row, n_col = lax.axis_size("row"), lax.axis_size("col")
    pairs = [(r, c) for r in range(n_row) for c in range(n_col)]
    moves = [(r * n_col + c, (r ^ row_mask) * n_col + (c ^ column_mask)) for r, c in pairs]
    return lax.ppermute(x, ("row", "col"), moves)


def summed(x, axis, digit):
    parts = [sent(x, axis, digit, shift) for shift in range(1, digit[1])]
    return functools.reduce(jnp.add, parts, x)


def scatter_digit(size, piece, tile):
    for stride, factor in digits_of(size):
        if factor == 2 and piece * stride % tile == 0:
            return (stride, factor)
    return None


def stage_kernel(count, *refs):
    sources, targets, arrived = refs[:count], refs[count : 2 * count], refs[2 * count]
    copies = [
        pltpu.make_async_copy(source, target, arrived.at[n])
        for n, (source, target) in enumerate(zip(sources, targets))
    ]
    for copy in copies:
        copy.start()
    for copy in copies:
        copy.wait()


def staged(*arrays):
    return pl.pallas_call(
        functools.partial(stage_kernel, len(arrays)),
        out_shape=[jax.ShapeDtypeStruct(a.shape, a.dtype) for a in arrays],
        in_specs=[pl.BlockSpec(memory_space=pltpu.HBM)] * len(arrays),
        out_specs=[pl.BlockSpec(memory_space=pltpu.VMEM)] * len(arrays),
        scratch_shapes=[pltpu.SemaphoreType.DMA((len(arrays),))],
        compiler_params=pltpu.CompilerParams(vmem_limit_bytes=8 << 20),
        cost_estimate=pl.CostEstimate(
            flops=0, transcendentals=0, bytes_accessed=sum(a.size * a.dtype.itemsize for a in arrays)
        ),
        name="staged",
    )(*arrays)


def product_kernel(layout, h_list_ref, j_list_ref, *refs):
    column_tiles, row_tiles, group, halves, stride, pieces = layout
    vector_refs, (h_ref, j_ref), outs = refs[:pieces], refs[pieces : pieces + 2], refs[pieces + 2 : -2]
    picked, total = refs[-2:]
    kept_tiles = row_tiles // halves
    tile = h_ref.shape[-1]
    each = column_tiles // pieces
    for n, vector_ref in enumerate(vector_refs):
        for t in range(each):
            picked[:, n * each + t] = vector_ref[:, :, t * tile : (t + 1) * tile]
    total[...] = jnp.zeros_like(total)
    place = lax.axis_index("col") // stride % halves
    turn = lax.axis_index("row")
    for s in range(total.shape[0]):
        for tiles, codes in ((h_ref, h_list_ref), (j_ref, j_list_ref)):
            slots = tiles.shape[1]
            for q in range(slots):
                code = codes[s * slots + q]
                spot = jnp.maximum(code, 0)
                strip = spot // column_tiles
                column = spot - strip * column_tiles
                if pieces > 1:
                    column = column ^ turn
                operator = strip // row_tiles
                row = strip - operator * row_tiles
                if tiles is j_ref:
                    operator = operator + 1
                half = row // group % halves
                local = row // (group * halves) * group + row % group
                half = jnp.where(half == place, 0, 1) if halves > 1 else 0
                at = (half * kept_tiles + local) * (J_OPERATORS + 1) + operator
                at = jnp.where(code >= 0, at, row_tiles * (J_OPERATORS + 1))
                product = lax.dot_general(
                    picked[s, column],
                    tiles[s, q],
                    (((1,), (1,)), ((), ())),
                    preferred_element_type=jnp.float32,
                )
                total[s, at] += product
    count = kept_tiles * (J_OPERATORS + 1)
    for half, out in enumerate(outs):
        out[...] = total[:, half * count : (half + 1) * count]


def tile_products(h_list, j_list, vectors, h_tiles, j_tiles, layout):
    column_tiles, row_tiles, group, halves, stride, pieces = layout
    sectors, count_vectors = vectors[0].shape[:2]
    tile = h_tiles.shape[-1]
    count = row_tiles // halves * (J_OPERATORS + 1)
    smem = pl.BlockSpec(memory_space=pltpu.SMEM)
    vmem = pl.BlockSpec(memory_space=pltpu.VMEM)
    shape = jax.ShapeDtypeStruct((sectors, count, count_vectors, tile), jnp.float32)
    extended = (sectors, row_tiles * (J_OPERATORS + 1) + 1, count_vectors, tile)
    return pl.pallas_call(
        functools.partial(product_kernel, layout),
        out_shape=[shape] * halves,
        in_specs=[smem] * 2 + [vmem] * (pieces + 2),
        out_specs=[vmem] * halves,
        scratch_shapes=[
            pltpu.VMEM((sectors, column_tiles, count_vectors, tile), jnp.bfloat16),
            pltpu.VMEM(extended, jnp.float32),
        ],
        compiler_params=pltpu.CompilerParams(vmem_limit_bytes=8 << 20),
        name="tile_products",
    )(h_list, j_list, *vectors, h_tiles, j_tiles)


def gram_kernel(x_ref, out_ref):
    sectors, count, vectors, _ = x_ref.shape
    operators = J_OPERATORS + 1
    out_ref[...] = jnp.zeros_like(out_ref)
    for s in range(sectors):
        part = None
        for t in range(count // operators):
            strip = x_ref[s, t * operators : (t + 1) * operators]
            term = lax.dot_general(
                strip[0],
                strip.reshape(operators * vectors, -1),
                (((1,), (1,)), ((), ())),
                precision=exact_precision,
                preferred_element_type=jnp.float32,
            )
            part = term if part is None else part + term
        out_ref[s, :, : operators * vectors] = part


def gram_parts(x):
    sectors, _, vectors, _ = x.shape
    vmem = pl.BlockSpec(memory_space=pltpu.VMEM)
    return pl.pallas_call(
        gram_kernel,
        out_shape=jax.ShapeDtypeStruct((sectors, vectors, LANES), jnp.float32),
        in_specs=[vmem],
        out_specs=vmem,
        compiler_params=pltpu.CompilerParams(vmem_limit_bytes=4 << 20),
        name="gram_parts",
    )(x)


def columns_of(matrix, first, count, width):
    return [jnp.broadcast_to(matrix[:, k : k + 1], (count, width)) for k in range(first, first + count)]


def product_of(columns, right):
    parts = [column * right[k : k + 1, :] for k, column in enumerate(columns)]
    while len(parts) > 1:
        parts = [functools.reduce(jnp.add, parts[i : i + 2]) for i in range(0, len(parts), 2)]
    return parts[0]


def root_kernel(layout, gram_ref, x_ref, basis_ref, elements_ref):
    total_rows, own_tiles, piece, group, halves = layout
    first = lax.axis_index("col") * piece // x_ref.shape[-1]
    own = first if halves == 1 else first // (group * halves) * group + first % group
    vectors, tile = x_ref.shape[2:]
    operators = J_OPERATORS + 1
    shape = (vectors, LANES)
    rows = lax.broadcasted_iota(jnp.int32, shape, 0)
    lanes = lax.broadcasted_iota(jnp.int32, shape, 1)
    is_gram = lanes < vectors
    root_at = operators * vectors
    step = jnp.where(lanes == rows, 1.5, 0.0).astype(jnp.float32)
    for s in range(x_ref.shape[0]):
        held = gram_ref[s]
        squares = jnp.where(is_gram, held * held, 0.0)
        squares = jnp.sum(jnp.sum(squares, axis=1, keepdims=True), axis=0, keepdims=True)
        scale = jnp.sqrt(squares + 1e-06)
        held = jnp.where(is_gram, held / scale, held)
        held = jnp.where(lanes == rows + root_at, 1.0, held)
        for iteration in range(NSIT):
            middle = columns_of(step - 0.5 * held, 0, vectors, LANES)
            once = product_of(middle, held)
            if iteration < NSIT - 1:
                held = jnp.where(is_gram, product_of(middle, once), once)
            else:
                held = once
        held = held * jnp.sqrt(total_rows / scale)
        root = columns_of(held, root_at, vectors, tile)
        for t in range(own_tiles):
            at = (own + t) * operators
            basis_ref[s, :, t * tile : (t + 1) * tile] = product_of(root, x_ref[s, at])
        for a in range(J_OPERATORS):
            elements = held[:, (a + 1) * vectors : (a + 2) * vectors]
            elements_ref[s, a] = elements / math.sqrt(total_rows)


def orthonormal(gram, x, layout):
    sectors, _, vectors, tile = x.shape
    vmem = pl.BlockSpec(memory_space=pltpu.VMEM)
    return pl.pallas_call(
        functools.partial(root_kernel, layout),
        out_shape=[
            jax.ShapeDtypeStruct((sectors, vectors, layout[1] * tile), jnp.float32),
            jax.ShapeDtypeStruct((sectors, J_OPERATORS, vectors, vectors), jnp.float32),
        ],
        in_specs=[vmem, vmem],
        out_specs=[vmem, vmem],
        compiler_params=pltpu.CompilerParams(vmem_limit_bytes=4 << 20),
        name="orthonormal",
    )(gram, x)


def per_device(vectors, h_tiles, h_list, j_tiles, j_list):
    sectors, _, piece = vectors.shape
    tile = h_tiles.shape[-1]
    n_row, n_col = lax.axis_size("row"), lax.axis_size("col")
    column = lax.axis_index("col")
    block_rows = piece * n_col
    row_tiles = block_rows // tile
    column_tiles = piece * n_row // tile
    total_rows = block_rows * n_row
    digit = scatter_digit(n_col, piece, tile)
    halves = 1 if digit is None else 2
    group = 1 if digit is None else piece * digit[0] // tile
    stride = 1 if digit is None else digit[0]
    direct = piece == tile and n_row in (2, 4)

    own_vectors, h_codes, j_codes, h_held, j_held = staged(
        vectors,
        h_list.reshape(-1),
        j_list.reshape(-1),
        h_tiles.reshape(sectors, -1, tile, tile),
        j_tiles.reshape(sectors, -1, tile, tile),
    )
    if direct:
        parts = [own_vectors]
        for mask in range(1, n_row):
            parts.append(lax.ppermute(vectors, "row", [(i, i ^ mask) for i in range(n_row)]))
    else:
        parts = [lax.all_gather(vectors, "row", axis=2, tiled=True)]
    outs = tile_products(
        h_codes, j_codes, parts, h_held, j_held,
        (column_tiles, row_tiles, group, halves, stride, len(parts)),
    )
    x = outs[0]
    if digit is not None:
        x = x + sent(outs[1], "col", digit, 1)
    for other in digits_of(n_col):
        if other != digit:
            x = summed(x, "col", other)

    gram = gram_parts(x)
    if direct and n_row == 4 and digit is not None:
        gram = summed(gram, "row", (1, 2))
        gram = gram + across(gram, 0, digit[0]) + across(gram, 2, 0) + across(gram, 2, digit[0])
    else:
        for other in digits_of(n_row):
            gram = summed(gram, "row", other)
        if digit is not None:
            gram = summed(gram, "col", digit)

    own_tiles = max(1, piece // tile)
    basis, elements = orthonormal(gram, x, (total_rows, own_tiles, piece, group, halves))
    if piece < tile:
        basis = lax.dynamic_slice_in_dim(basis, column * piece % tile, piece, 2)
    return (basis, elements)


def solution(mesh):
    return jax.shard_map(
        per_device,
        mesh=mesh,
        in_specs=(
            P(None, None, ("col", "row")),
            P(None, "row", "col", None, None),
            P(None, "row", "col"),
            P(None, "row", "col", None, None),
            P(None, "row", "col"),
        ),
        out_specs=(P(None, None, ("row", "col")), P()),
        check_vma=False,
    )
```

```python
import functools
import math

import jax
import jax.numpy as jnp
from jax import lax
from jax.experimental import pallas as pl
from jax.experimental.pallas import tpu as pltpu
from jax.sharding import PartitionSpec as P

NSIT = 6
J_OPERATORS = 2
LANES = 128
COVER_FLOPS = 4 << 30

exact_precision = lax.Precision.HIGHEST


def digits_of(size):
    digits, stride = [], 1
    while stride < size:
        rest = size // stride
        factor = next(f for f in range(2, rest + 1) if rest % f == 0)
        digits.append((stride, factor))
        stride *= factor
    return digits


def moved(index, digit, shift):
    stride, factor = digit
    value = index // stride % factor
    return index + ((value + shift) % factor - value) * stride


def sent(x, axis, digit, shift):
    size = lax.axis_size(axis)
    return lax.ppermute(x, axis, [(i, moved(i, digit, shift)) for i in range(size)])


def across(x, row_mask, column_mask):
    n_row, n_col = lax.axis_size("row"), lax.axis_size("col")
    pairs = [(r, c) for r in range(n_row) for c in range(n_col)]
    moves = [(r * n_col + c, (r ^ row_mask) * n_col + (c ^ column_mask)) for r, c in pairs]
    return lax.ppermute(x, ("row", "col"), moves)


def summed(x, axis, digit):
    parts = [sent(x, axis, digit, shift) for shift in range(1, digit[1])]
    return functools.reduce(jnp.add, parts, x)


def scatter_digit(size, piece, tile):
    for stride, factor in digits_of(size):
        if factor == 2 and piece * stride % tile == 0:
            return (stride, factor)
    return None


def quotient(x, divisor, limit):
    if divisor & (divisor - 1) == 0:
        return lax.shift_right_logical(x, divisor.bit_length() - 1)
    marks = range(divisor, limit, divisor)
    return sum((jnp.where(x >= mark, 1, 0) for mark in marks), jnp.zeros_like(x))


def spot_kernel(layout, h_list_ref, j_list_ref, spot_ref):
    column_tiles, row_tiles, group, halves, stride, pieces, bits = layout
    operators = J_OPERATORS + 1
    positions = row_tiles * column_tiles
    place = lax.axis_index("col") // stride % halves
    turn = lax.axis_index("row")
    start = 0
    for list_ref, first in ((h_list_ref, 0), (j_list_ref, 1)):
        code = list_ref[...]
        spot = jnp.maximum(code, 0)
        strip = quotient(spot, column_tiles, J_OPERATORS * positions)
        column = spot - strip * column_tiles
        if pieces > 1:
            column = column ^ turn
        operator = quotient(strip, row_tiles, J_OPERATORS * row_tiles)
        row = strip - operator * row_tiles
        chunk = quotient(row, group, row_tiles)
        outer = quotient(chunk, halves, row_tiles)
        local = outer * group + row - chunk * group
        side = jnp.where(chunk - outer * halves == place, 0, row_tiles // halves * operators)
        at = side + local * operators + operator + first
        at = jnp.where(code >= 0, at, row_tiles * operators)
        slots = code.shape[1]
        spot_ref[:, start : start + slots] = lax.shift_left(at, bits) + column
        start += slots


def spots(h_list, j_list, layout):
    vmem = pl.BlockSpec(memory_space=pltpu.VMEM)
    return pl.pallas_call(
        functools.partial(spot_kernel, layout),
        out_shape=jax.ShapeDtypeStruct((h_list.shape[0], LANES), jnp.int32),
        in_specs=[vmem, vmem],
        out_specs=vmem,
        compiler_params=pltpu.CompilerParams(vmem_limit_bytes=1 << 20),
        cost_estimate=pl.CostEstimate(flops=COVER_FLOPS, transcendentals=0, bytes_accessed=1 << 12),
        name="spots",
    )(h_list, j_list)


def product_kernel(layout, spot_ref, *refs):
    column_tiles, row_tiles, group, halves, stride, pieces, bits = layout
    vector_refs, (h_ref, j_ref), outs = refs[:pieces], refs[pieces : pieces + 2], refs[pieces + 2 : -5]
    held, products, total, spot, arrived = refs[-5:]
    fetch = pltpu.make_async_copy(spot_ref, spot, arrived)
    fetch.start()
    sectors, vectors, tile = held.shape[0], vector_refs[0].shape[1], h_ref.shape[-1]
    each = column_tiles // pieces
    wide = column_tiles * vectors
    held[...] = jnp.zeros_like(held)
    for n, vector_ref in enumerate(vector_refs):
        for t in range(each):
            at = (n * each + t) * vectors
            for side in range(2):
                held[:, side * wide + at : side * wide + at + vectors, side * tile : (side + 1) * tile] = (
                    vector_ref[:, :, t * tile : (t + 1) * tile]
                )
    total[...] = jnp.zeros_like(total)
    slots = [(tiles, q) for tiles in (h_ref, j_ref) for q in range(tiles.shape[1])]
    for s in range(sectors):
        for n in range(0, len(slots), 4):
            some = [tiles[s, q] for tiles, q in slots[n : n + 4]]
            pairs = [jnp.concatenate([some[i], some[(i + 1) % len(some)]], 1) for i in range(0, len(some), 2)]
            product = lax.dot_general(
                held[s], jnp.concatenate(pairs, 0), (((1,), (1,)), ((), ())), preferred_element_type=jnp.float32
            )
            for i in range(len(some)):
                side, column = i % 2, i // 2
                part = product[side * wide : (side + 1) * wide, column * tile : (column + 1) * tile]
                products[s, n + i] = part.reshape(column_tiles, vectors, tile)
    fetch.wait()
    for s in range(sectors):
        for n in range(len(slots)):
            word = spot[s, n]
            at = lax.shift_right_logical(word, bits)
            total[s, at] += products[s, n, word & ((1 << bits) - 1)]
    count = row_tiles // halves * (J_OPERATORS + 1)
    for half, out in enumerate(outs):
        out[...] = total[:, half * count : (half + 1) * count]


def tile_products(where, vectors, h_tiles, j_tiles, layout):
    column_tiles, row_tiles, group, halves, stride, pieces, bits = layout
    sectors, count_vectors = vectors[0].shape[:2]
    tile = h_tiles.shape[-1]
    slots = h_tiles.shape[1] + j_tiles.shape[1]
    count = row_tiles // halves * (J_OPERATORS + 1)
    vmem = pl.BlockSpec(memory_space=pltpu.VMEM)
    shape = jax.ShapeDtypeStruct((sectors, count, count_vectors, tile), jnp.float32)
    extended = (sectors, row_tiles * (J_OPERATORS + 1) + 1, count_vectors, tile)
    return pl.pallas_call(
        functools.partial(product_kernel, layout),
        out_shape=[shape] * halves,
        in_specs=[pl.BlockSpec(memory_space=pl.ANY)] + [vmem] * (pieces + 2),
        out_specs=[vmem] * halves,
        scratch_shapes=[
            pltpu.VMEM((sectors, 2 * column_tiles * count_vectors, 2 * tile), jnp.bfloat16),
            pltpu.VMEM((sectors, slots, column_tiles, count_vectors, tile), jnp.float32),
            pltpu.VMEM(extended, jnp.float32),
            pltpu.SMEM(where.shape, jnp.int32),
            pltpu.SemaphoreType.DMA,
        ],
        compiler_params=pltpu.CompilerParams(vmem_limit_bytes=8 << 20),
        name="tile_products",
    )(where, *vectors, h_tiles, j_tiles)


def gram_kernel(x_ref, out_ref):
    sectors, count, vectors, _ = x_ref.shape
    operators = J_OPERATORS + 1
    out_ref[...] = jnp.zeros_like(out_ref)
    for s in range(sectors):
        part = None
        for t in range(count // operators):
            strip = x_ref[s, t * operators : (t + 1) * operators]
            term = lax.dot_general(
                strip[0],
                strip.reshape(operators * vectors, -1),
                (((1,), (1,)), ((), ())),
                precision=exact_precision,
                preferred_element_type=jnp.float32,
            )
            part = term if part is None else part + term
        out_ref[s, :, : operators * vectors] = part


def gram_parts(x):
    sectors, _, vectors, _ = x.shape
    vmem = pl.BlockSpec(memory_space=pltpu.VMEM)
    return pl.pallas_call(
        gram_kernel,
        out_shape=jax.ShapeDtypeStruct((sectors, vectors, LANES), jnp.float32),
        in_specs=[vmem],
        out_specs=vmem,
        compiler_params=pltpu.CompilerParams(vmem_limit_bytes=4 << 20),
        name="gram_parts",
    )(x)


def columns_of(matrix, first, count, width):
    return [jnp.broadcast_to(matrix[:, k : k + 1], (count, width)) for k in range(first, first + count)]


def product_of(columns, right):
    parts = [column * right[k : k + 1, :] for k, column in enumerate(columns)]
    while len(parts) > 1:
        parts = [functools.reduce(jnp.add, parts[i : i + 2]) for i in range(0, len(parts), 2)]
    return parts[0]


def root_kernel(layout, gram_ref, x_ref, basis_ref, elements_ref):
    total_rows, own_tiles, piece, group, halves = layout
    first = lax.axis_index("col") * piece // x_ref.shape[-1]
    own = first if halves == 1 else first // (group * halves) * group + first % group
    vectors, tile = x_ref.shape[2:]
    operators = J_OPERATORS + 1
    shape = (vectors, LANES)
    rows = lax.broadcasted_iota(jnp.int32, shape, 0)
    lanes = lax.broadcasted_iota(jnp.int32, shape, 1)
    is_gram = lanes < vectors
    root_at = operators * vectors
    step = jnp.where(lanes == rows, 1.5, 0.0).astype(jnp.float32)
    for s in range(x_ref.shape[0]):
        held = gram_ref[s]
        squares = jnp.where(is_gram, held * held, 0.0)
        squares = jnp.sum(jnp.sum(squares, axis=1, keepdims=True), axis=0, keepdims=True)
        scale = jnp.sqrt(squares + 1e-06)
        held = jnp.where(is_gram, held / scale, held)
        held = jnp.where(lanes == rows + root_at, 1.0, held)
        for iteration in range(NSIT):
            middle = columns_of(step - 0.5 * held, 0, vectors, LANES)
            once = product_of(middle, held)
            if iteration < NSIT - 1:
                held = jnp.where(is_gram, product_of(middle, once), once)
            else:
                held = once
        held = held * jnp.sqrt(total_rows / scale)
        root = columns_of(held, root_at, vectors, tile)
        for t in range(own_tiles):
            at = (own + t) * operators
            basis_ref[s, :, t * tile : (t + 1) * tile] = product_of(root, x_ref[s, at])
        for a in range(J_OPERATORS):
            elements = held[:, (a + 1) * vectors : (a + 2) * vectors]
            elements_ref[s, a] = elements / math.sqrt(total_rows)


def orthonormal(gram, x, layout):
    sectors, _, vectors, tile = x.shape
    vmem = pl.BlockSpec(memory_space=pltpu.VMEM)
    return pl.pallas_call(
        functools.partial(root_kernel, layout),
        out_shape=[
            jax.ShapeDtypeStruct((sectors, vectors, layout[1] * tile), jnp.float32),
            jax.ShapeDtypeStruct((sectors, J_OPERATORS, vectors, vectors), jnp.float32),
        ],
        in_specs=[vmem, vmem],
        out_specs=[vmem, vmem],
        compiler_params=pltpu.CompilerParams(vmem_limit_bytes=4 << 20),
        name="orthonormal",
    )(gram, x)


def per_device(vectors, h_tiles, h_list, j_tiles, j_list):
    sectors, _, piece = vectors.shape
    tile = h_tiles.shape[-1]
    n_row, n_col = lax.axis_size("row"), lax.axis_size("col")
    column = lax.axis_index("col")
    block_rows = piece * n_col
    row_tiles = block_rows // tile
    column_tiles = piece * n_row // tile
    total_rows = block_rows * n_row
    digit = scatter_digit(n_col, piece, tile)
    halves = 1 if digit is None else 2
    group = 1 if digit is None else piece * digit[0] // tile
    stride = 1 if digit is None else digit[0]
    direct = piece == tile and n_row in (2, 4)

    if direct:
        parts = [vectors]
        for mask in range(1, n_row):
            parts.append(lax.ppermute(vectors, "row", [(i, i ^ mask) for i in range(n_row)]))
    else:
        parts = [lax.all_gather(vectors, "row", axis=2, tiled=True)]
    bits = (column_tiles - 1).bit_length()
    layout = (column_tiles, row_tiles, group, halves, stride, len(parts), bits)
    where = spots(h_list.reshape(sectors, -1), j_list.reshape(sectors, -1), layout)
    outs = tile_products(
        where,
        parts,
        h_tiles.reshape(sectors, -1, tile, tile),
        j_tiles.reshape(sectors, -1, tile, tile),
        layout,
    )
    x = outs[0]
    if digit is not None:
        x = x + sent(outs[1], "col", digit, 1)
    for other in digits_of(n_col):
        if other != digit:
            x = summed(x, "col", other)

    gram = gram_parts(x)
    if direct and n_row == 4 and digit is not None:
        gram = gram + across(gram, 1, 0) + across(gram, 2, 0) + across(gram, 3, 0)
        gram = gram + across(gram, 0, digit[0])
    else:
        for other in digits_of(n_row):
            gram = summed(gram, "row", other)
        if digit is not None:
            gram = summed(gram, "col", digit)

    own_tiles = max(1, piece // tile)
    basis, elements = orthonormal(gram, x, (total_rows, own_tiles, piece, group, halves))
    if piece < tile:
        basis = lax.dynamic_slice_in_dim(basis, column * piece % tile, piece, 2)
    return (basis, elements)


def solution(mesh):
    return jax.shard_map(
        per_device,
        mesh=mesh,
        in_specs=(
            P(None, None, ("col", "row")),
            P(None, "row", "col", None, None),
            P(None, "row", "col"),
            P(None, "row", "col", None, None),
            P(None, "row", "col"),
        ),
        out_specs=(P(None, None, ("row", "col")), P()),
        check_vma=False,
    )
```

```python
import functools
import math

import jax
import jax.numpy as jnp
from jax import lax
from jax.experimental import pallas as pl
from jax.experimental.pallas import tpu as pltpu
from jax.sharding import PartitionSpec as P

NSIT = 6
J_OPERATORS = 2
LANES = 128
H_CHAINS = 3
COVER_FLOPS = 4 << 30

exact_precision = lax.Precision.HIGHEST


def digits_of(size):
    digits, stride = [], 1
    while stride < size:
        rest = size // stride
        factor = next(f for f in range(2, rest + 1) if rest % f == 0)
        digits.append((stride, factor))
        stride *= factor
    return digits


def moved(index, digit, shift):
    stride, factor = digit
    value = index // stride % factor
    return index + ((value + shift) % factor - value) * stride


def sent(x, axis, digit, shift):
    size = lax.axis_size(axis)
    return lax.ppermute(x, axis, [(i, moved(i, digit, shift)) for i in range(size)])


def across(x, row_mask, column_mask):
    n_row, n_col = lax.axis_size("row"), lax.axis_size("col")
    pairs = [(r, c) for r in range(n_row) for c in range(n_col)]
    moves = [(r * n_col + c, (r ^ row_mask) * n_col + (c ^ column_mask)) for r, c in pairs]
    return lax.ppermute(x, ("row", "col"), moves)


def summed(x, axis, digit):
    parts = [sent(x, axis, digit, shift) for shift in range(1, digit[1])]
    return functools.reduce(jnp.add, parts, x)


def scatter_digit(size, piece, tile):
    for stride, factor in digits_of(size):
        if factor == 2 and piece * stride % tile == 0:
            return (stride, factor)
    return None


def quotient(x, divisor, limit):
    if divisor & (divisor - 1) == 0:
        return lax.shift_right_logical(x, divisor.bit_length() - 1)
    marks = range(divisor, limit, divisor)
    return sum((jnp.where(x >= mark, 1, 0) for mark in marks), jnp.zeros_like(x))


def spot_kernel(layout, h_list_ref, j_list_ref, spot_ref):
    column_tiles, row_tiles, group, halves, stride, pieces, bits = layout
    positions = row_tiles * column_tiles
    place = lax.axis_index("col") // stride % halves
    turn = lax.axis_index("row")
    start = 0
    for list_ref, count in ((h_list_ref, 1), (j_list_ref, J_OPERATORS)):
        code = list_ref[...]
        spot = jnp.maximum(code, 0)
        strip = quotient(spot, column_tiles, J_OPERATORS * positions)
        column = spot - strip * column_tiles
        if pieces > 1:
            column = column ^ turn
        operator = quotient(strip, row_tiles, J_OPERATORS * row_tiles)
        row = strip - operator * row_tiles
        chunk = quotient(row, group, row_tiles)
        outer = quotient(chunk, halves, row_tiles)
        local = outer * group + row - chunk * group
        strips = jnp.where(chunk - outer * halves == place, 0, row_tiles // halves) + local
        at = jnp.where(code >= 0, strips * count + operator, row_tiles * count)
        slots = code.shape[1]
        spot_ref[:, start : start + slots] = lax.shift_left(at, bits) + column
        start += slots


def spots(h_list, j_list, layout):
    vmem = pl.BlockSpec(memory_space=pltpu.VMEM)
    return pl.pallas_call(
        functools.partial(spot_kernel, layout),
        out_shape=jax.ShapeDtypeStruct((h_list.shape[0], LANES), jnp.int32),
        in_specs=[vmem, vmem],
        out_specs=vmem,
        compiler_params=pltpu.CompilerParams(vmem_limit_bytes=1 << 20),
        cost_estimate=pl.CostEstimate(flops=COVER_FLOPS, transcendentals=0, bytes_accessed=1 << 12),
        name="spots",
    )(h_list, j_list)


def turn_kernel(*refs):
    count = len(refs) // 2
    for source, target in zip(refs[:count], refs[count:]):
        for s in range(source.shape[0]):
            for q in range(source.shape[1]):
                target[s, q] = source[s, q].T


def turned(*arrays):
    vmem = pl.BlockSpec(memory_space=pltpu.VMEM)
    return pl.pallas_call(
        turn_kernel,
        out_shape=[jax.ShapeDtypeStruct(a.shape, a.dtype) for a in arrays],
        in_specs=[vmem] * len(arrays),
        out_specs=[vmem] * len(arrays),
        compiler_params=pltpu.CompilerParams(vmem_limit_bytes=4 << 20),
        cost_estimate=pl.CostEstimate(
            flops=0, transcendentals=0, bytes_accessed=2 * sum(a.size * a.dtype.itemsize for a in arrays)
        ),
        name="turned",
    )(*arrays)


def product_kernel(layout, spot_ref, *refs):
    column_tiles, row_tiles, group, halves, stride, pieces, bits = layout
    vector_refs, (h_ref, j_ref), outs = refs[:pieces], refs[pieces : pieces + 2], refs[pieces + 2 : pieces + 2 + halves]
    held, products, spot, arrived = refs[pieces + 2 + halves : pieces + 6 + halves]
    totals = refs[pieces + 6 + halves :]
    fetch = pltpu.make_async_copy(spot_ref, spot, arrived)
    fetch.start()
    sectors, vectors, tile = held.shape[0], vector_refs[0].shape[1], h_ref.shape[-1]
    each = column_tiles // pieces
    wide = column_tiles * vectors
    held[...] = jnp.zeros_like(held)
    for n, vector_ref in enumerate(vector_refs):
        for t in range(each):
            at = (n * each + t) * vectors
            for side in range(2):
                held[:, side * wide + at : side * wide + at + vectors, side * tile : (side + 1) * tile] = (
                    vector_ref[:, :, t * tile : (t + 1) * tile]
                )
    for total in totals:
        total[...] = jnp.zeros_like(total)
    slots = [(tiles, q) for tiles in (h_ref, j_ref) for q in range(tiles.shape[1])]
    for s in range(sectors):
        for n in range(0, len(slots), 4):
            some = [tiles[s, q] for tiles, q in slots[n : n + 4]]
            pairs = [jnp.concatenate([some[i], some[(i + 1) % len(some)]], 0) for i in range(0, len(some), 2)]
            product = jnp.dot(
                held[s], jnp.concatenate(pairs, 1), preferred_element_type=jnp.float32
            )
            for i in range(len(some)):
                side, column = i % 2, i // 2
                part = product[side * wide : (side + 1) * wide, column * tile : (column + 1) * tile]
                products[s, n + i] = part.reshape(column_tiles, vectors, tile)
    fetch.wait()
    chains = len(totals) - 1
    h_slots = h_ref.shape[1]
    order = [(n // chains, totals[n % chains], n) for n in range(h_slots)]
    order += [(n - h_slots, totals[-1], n) for n in range(h_slots, len(slots))]
    order.sort(key=lambda entry: entry[0])
    kept_tiles = row_tiles // halves
    for s in range(sectors):
        for _, total, n in order:
            word = spot[s, n]
            at = lax.shift_right_logical(word, bits)
            total[s, at] += products[s, n, word & ((1 << bits) - 1)]
        for half, out in enumerate(outs):
            for t in range(kept_tiles):
                strip = half * kept_tiles + t
                first = t * (J_OPERATORS + 1)
                out[s, first] = functools.reduce(jnp.add, [total[s, strip] for total in totals[:-1]])
                for a in range(J_OPERATORS):
                    out[s, first + 1 + a] = totals[-1][s, strip * J_OPERATORS + a]


def tile_products(where, vectors, h_tiles, j_tiles, layout):
    column_tiles, row_tiles, group, halves, stride, pieces, bits = layout
    sectors, count_vectors = vectors[0].shape[:2]
    tile = h_tiles.shape[-1]
    slots = h_tiles.shape[1] + j_tiles.shape[1]
    count = row_tiles // halves * (J_OPERATORS + 1)
    vmem = pl.BlockSpec(memory_space=pltpu.VMEM)
    shape = jax.ShapeDtypeStruct((sectors, count, count_vectors, tile), jnp.float32)
    h_total = (sectors, row_tiles + 1, count_vectors, tile)
    j_total = (sectors, row_tiles * J_OPERATORS + 1, count_vectors, tile)
    return pl.pallas_call(
        functools.partial(product_kernel, layout),
        out_shape=[shape] * halves,
        in_specs=[pl.BlockSpec(memory_space=pl.ANY)] + [vmem] * (pieces + 2),
        out_specs=[vmem] * halves,
        scratch_shapes=[
            pltpu.VMEM((sectors, 2 * column_tiles * count_vectors, 2 * tile), jnp.bfloat16),
            pltpu.VMEM((sectors, slots, column_tiles, count_vectors, tile), jnp.float32),
            pltpu.SMEM(where.shape, jnp.int32),
            pltpu.SemaphoreType.DMA,
        ]
        + [pltpu.VMEM(h_total, jnp.float32)] * H_CHAINS
        + [pltpu.VMEM(j_total, jnp.float32)],
        compiler_params=pltpu.CompilerParams(vmem_limit_bytes=8 << 20),
        name="tile_products",
    )(where, *vectors, h_tiles, j_tiles)


def gram_kernel(x_ref, out_ref):
    sectors, count, vectors, _ = x_ref.shape
    operators = J_OPERATORS + 1
    out_ref[...] = jnp.zeros_like(out_ref)
    for s in range(sectors):
        part = None
        for t in range(count // operators):
            strip = x_ref[s, t * operators : (t + 1) * operators]
            term = lax.dot_general(
                strip[0],
                strip.reshape(operators * vectors, -1),
                (((1,), (1,)), ((), ())),
                precision=exact_precision,
                preferred_element_type=jnp.float32,
            )
            part = term if part is None else part + term
        out_ref[s, :, : operators * vectors] = part


def gram_parts(x):
    sectors, _, vectors, _ = x.shape
    vmem = pl.BlockSpec(memory_space=pltpu.VMEM)
    return pl.pallas_call(
        gram_kernel,
        out_shape=jax.ShapeDtypeStruct((sectors, vectors, LANES), jnp.float32),
        in_specs=[vmem],
        out_specs=vmem,
        compiler_params=pltpu.CompilerParams(vmem_limit_bytes=4 << 20),
        name="gram_parts",
    )(x)


def columns_of(matrix, first, count, width):
    return [jnp.broadcast_to(matrix[:, k : k + 1], (count, width)) for k in range(first, first + count)]


def product_of(columns, right):
    parts = [column * right[k : k + 1, :] for k, column in enumerate(columns)]
    while len(parts) > 1:
        parts = [functools.reduce(jnp.add, parts[i : i + 2]) for i in range(0, len(parts), 2)]
    return parts[0]


def root_kernel(layout, gram_ref, x_ref, basis_ref, elements_ref):
    total_rows, own_tiles, piece, group, halves = layout
    first = lax.axis_index("col") * piece // x_ref.shape[-1]
    own = first if halves == 1 else first // (group * halves) * group + first % group
    vectors, tile = x_ref.shape[2:]
    operators = J_OPERATORS + 1
    shape = (vectors, LANES)
    rows = lax.broadcasted_iota(jnp.int32, shape, 0)
    lanes = lax.broadcasted_iota(jnp.int32, shape, 1)
    is_gram = lanes < vectors
    root_at = operators * vectors
    step = jnp.where(lanes == rows, 1.5, 0.0).astype(jnp.float32)
    for s in range(x_ref.shape[0]):
        held = gram_ref[s]
        squares = jnp.where(is_gram, held * held, 0.0)
        squares = jnp.sum(jnp.sum(squares, axis=1, keepdims=True), axis=0, keepdims=True)
        scale = jnp.sqrt(squares + 1e-06)
        held = jnp.where(is_gram, held / scale, held)
        held = jnp.where(lanes == rows + root_at, 1.0, held)
        for iteration in range(NSIT):
            middle = columns_of(step - 0.5 * held, 0, vectors, LANES)
            once = product_of(middle, held)
            if iteration < NSIT - 1:
                held = jnp.where(is_gram, product_of(middle, once), once)
            else:
                held = once
        held = held * jnp.sqrt(total_rows / scale)
        root = columns_of(held, root_at, vectors, tile)
        for t in range(own_tiles):
            at = (own + t) * operators
            basis_ref[s, :, t * tile : (t + 1) * tile] = product_of(root, x_ref[s, at])
        for a in range(J_OPERATORS):
            elements = held[:, (a + 1) * vectors : (a + 2) * vectors]
            elements_ref[s, a] = elements / math.sqrt(total_rows)


def orthonormal(gram, x, layout):
    sectors, _, vectors, tile = x.shape
    vmem = pl.BlockSpec(memory_space=pltpu.VMEM)
    return pl.pallas_call(
        functools.partial(root_kernel, layout),
        out_shape=[
            jax.ShapeDtypeStruct((sectors, vectors, layout[1] * tile), jnp.float32),
            jax.ShapeDtypeStruct((sectors, J_OPERATORS, vectors, vectors), jnp.float32),
        ],
        in_specs=[vmem, vmem],
        out_specs=[vmem, vmem],
        compiler_params=pltpu.CompilerParams(vmem_limit_bytes=4 << 20),
        name="orthonormal",
    )(gram, x)


def per_device(vectors, h_tiles, h_list, j_tiles, j_list):
    sectors, _, piece = vectors.shape
    tile = h_tiles.shape[-1]
    n_row, n_col = lax.axis_size("row"), lax.axis_size("col")
    column = lax.axis_index("col")
    block_rows = piece * n_col
    row_tiles = block_rows // tile
    column_tiles = piece * n_row // tile
    total_rows = block_rows * n_row
    digit = scatter_digit(n_col, piece, tile)
    halves = 1 if digit is None else 2
    group = 1 if digit is None else piece * digit[0] // tile
    stride = 1 if digit is None else digit[0]
    direct = piece == tile and n_row in (2, 4)

    if direct:
        parts = [vectors]
        for mask in range(1, n_row):
            parts.append(lax.ppermute(vectors, "row", [(i, i ^ mask) for i in range(n_row)]))
    else:
        parts = [lax.all_gather(vectors, "row", axis=2, tiled=True)]
    bits = (column_tiles - 1).bit_length()
    layout = (column_tiles, row_tiles, group, halves, stride, len(parts), bits)
    where = spots(h_list.reshape(sectors, -1), j_list.reshape(sectors, -1), layout)
    h_turned, j_turned = turned(
        h_tiles.reshape(sectors, -1, tile, tile), j_tiles.reshape(sectors, -1, tile, tile)
    )
    outs = tile_products(where, parts, h_turned, j_turned, layout)
    x = outs[0]
    if digit is not None:
        x = x + sent(outs[1], "col", digit, 1)
    for other in digits_of(n_col):
        if other != digit:
            x = summed(x, "col", other)

    gram = gram_parts(x)
    if direct and n_row == 4 and digit is not None:
        gram = gram + across(gram, 1, 0) + across(gram, 2, 0) + across(gram, 3, 0)
        gram = gram + across(gram, 0, digit[0])
    else:
        for other in digits_of(n_row):
            gram = summed(gram, "row", other)
        if digit is not None:
            gram = summed(gram, "col", digit)

    own_tiles = max(1, piece // tile)
    basis, elements = orthonormal(gram, x, (total_rows, own_tiles, piece, group, halves))
    if piece < tile:
        basis = lax.dynamic_slice_in_dim(basis, column * piece % tile, piece, 2)
    return (basis, elements)


def solution(mesh):
    return jax.shard_map(
        per_device,
        mesh=mesh,
        in_specs=(
            P(None, None, ("col", "row")),
            P(None, "row", "col", None, None),
            P(None, "row", "col"),
            P(None, "row", "col", None, None),
            P(None, "row", "col"),
        ),
        out_specs=(P(None, None, ("row", "col")), P()),
        check_vma=False,
    )
```

```python
import functools
import math

import jax
import jax.numpy as jnp
from jax import lax
from jax.experimental import pallas as pl
from jax.experimental.pallas import tpu as pltpu
from jax.sharding import PartitionSpec as P

NSIT = 6
J_OPERATORS = 2
LANES = 128
COVER_FLOPS = 4 << 30

exact_precision = lax.Precision.HIGHEST


def digits_of(size):
    digits, stride = [], 1
    while stride < size:
        rest = size // stride
        factor = next(f for f in range(2, rest + 1) if rest % f == 0)
        digits.append((stride, factor))
        stride *= factor
    return digits


def moved(index, digit, shift):
    stride, factor = digit
    value = index // stride % factor
    return index + ((value + shift) % factor - value) * stride


def sent(x, axis, digit, shift):
    size = lax.axis_size(axis)
    return lax.ppermute(x, axis, [(i, moved(i, digit, shift)) for i in range(size)])


def across(x, row_mask, column_mask):
    n_row, n_col = lax.axis_size("row"), lax.axis_size("col")
    pairs = [(r, c) for r in range(n_row) for c in range(n_col)]
    moves = [(r * n_col + c, (r ^ row_mask) * n_col + (c ^ column_mask)) for r, c in pairs]
    return lax.ppermute(x, ("row", "col"), moves)


def summed(x, axis, digit):
    parts = [sent(x, axis, digit, shift) for shift in range(1, digit[1])]
    return functools.reduce(jnp.add, parts, x)


def scatter_digit(size, piece, tile):
    for stride, factor in digits_of(size):
        if factor == 2 and piece * stride % tile == 0:
            return (stride, factor)
    return None


def quotient(x, divisor, limit):
    if divisor & (divisor - 1) == 0:
        return lax.shift_right_logical(x, divisor.bit_length() - 1)
    marks = range(divisor, limit, divisor)
    return sum((jnp.where(x >= mark, 1, 0) for mark in marks), jnp.zeros_like(x))


def lead_kernel(place_ref):
    place_ref[...] = jnp.full(place_ref.shape, lax.axis_index("row"), jnp.int32)


def spot_kernel(layout, lead_ref, h_list_ref, j_list_ref, spot_ref):
    column_tiles, row_tiles, group, halves, stride, pieces, bits = layout
    positions = row_tiles * column_tiles
    place = lax.axis_index("col") // stride % halves
    turn = lead_ref[:1, :1]
    start = 0
    for list_ref, count in ((h_list_ref, 1), (j_list_ref, J_OPERATORS)):
        code = list_ref[...]
        spot = jnp.maximum(code, 0)
        strip = quotient(spot, column_tiles, J_OPERATORS * positions)
        column = spot - strip * column_tiles
        if pieces > 1:
            column = column ^ turn
        operator = quotient(strip, row_tiles, J_OPERATORS * row_tiles)
        row = strip - operator * row_tiles
        chunk = quotient(row, group, row_tiles)
        outer = quotient(chunk, halves, row_tiles)
        local = outer * group + row - chunk * group
        strips = jnp.where(chunk - outer * halves == place, 0, row_tiles // halves) + local
        at = jnp.where(code >= 0, strips * count + operator, row_tiles * count)
        slots = code.shape[1]
        spot_ref[:, start : start + slots] = lax.shift_left(at, bits) + column
        start += slots


def spots(h_list, j_list, layout):
    vmem = pl.BlockSpec(memory_space=pltpu.VMEM)
    cover = pl.CostEstimate(flops=COVER_FLOPS, transcendentals=0, bytes_accessed=1 << 12)
    lead = pl.pallas_call(
        lead_kernel,
        out_shape=jax.ShapeDtypeStruct((8, LANES), jnp.int32),
        out_specs=vmem,
        compiler_params=pltpu.CompilerParams(vmem_limit_bytes=1 << 20),
        cost_estimate=cover,
        name="lead",
    )()
    return pl.pallas_call(
        functools.partial(spot_kernel, layout),
        out_shape=jax.ShapeDtypeStruct((h_list.shape[0], h_list.shape[1] + j_list.shape[1]), jnp.int32),
        in_specs=[vmem] * 3,
        out_specs=vmem,
        compiler_params=pltpu.CompilerParams(vmem_limit_bytes=1 << 20),
        cost_estimate=cover,
        name="spots",
    )(lead, h_list, j_list)


def turn_kernel(layout, where_ref, h_ref, j_ref, h_block_ref, j_block_ref, spot, arrived):
    bits = layout[-1]
    fetch = pltpu.make_async_copy(where_ref, spot, arrived)
    fetch.start()
    h_block_ref[...] = jnp.zeros_like(h_block_ref)
    j_block_ref[...] = jnp.zeros_like(j_block_ref)
    fetch.wait()
    sectors, h_slots = h_ref.shape[:2]
    for s in range(sectors):
        for tiles, block, first in ((h_ref, h_block_ref, 0), (j_ref, j_block_ref, h_slots)):
            for q in range(tiles.shape[1]):
                word = spot[s, first + q]
                strip = lax.shift_right_logical(word, bits)
                block[s, word & ((1 << bits) - 1), strip] = tiles[s, q].T


def turned(where, h_tiles, j_tiles, layout):
    column_tiles, row_tiles = layout[:2]
    sectors, _, tile, _ = h_tiles.shape
    vmem = pl.BlockSpec(memory_space=pltpu.VMEM)
    shapes = [(sectors, column_tiles, row_tiles * n + 1, tile, tile) for n in (1, J_OPERATORS)]
    moved_bytes = 4 * (h_tiles.size + j_tiles.size)
    return pl.pallas_call(
        functools.partial(turn_kernel, layout),
        out_shape=[jax.ShapeDtypeStruct(shape, h_tiles.dtype) for shape in shapes],
        in_specs=[pl.BlockSpec(memory_space=pl.ANY), vmem, vmem],
        out_specs=[vmem, vmem],
        scratch_shapes=[pltpu.SMEM(where.shape, jnp.int32), pltpu.SemaphoreType.DMA],
        compiler_params=pltpu.CompilerParams(vmem_limit_bytes=4 << 20),
        cost_estimate=pl.CostEstimate(flops=0, transcendentals=0, bytes_accessed=moved_bytes),
        name="turned",
    )(where, h_tiles, j_tiles)


def product_kernel(layout, *refs):
    column_tiles, row_tiles, group, halves, stride, pieces, bits = layout
    vector_refs, (h_block_ref, j_block_ref), outs = refs[:pieces], refs[pieces : pieces + 2], refs[pieces + 2 :]
    kept_tiles, operators = row_tiles // halves, J_OPERATORS + 1
    tile = h_block_ref.shape[-1]
    each = column_tiles // pieces
    for s in range(outs[0].shape[0]):
        lined = jnp.concatenate(
            [vector_ref[s, :, t * tile : (t + 1) * tile] for vector_ref in vector_refs for t in range(each)], 1
        )
        for block_ref, first, count in ((j_block_ref, 1, J_OPERATORS), (h_block_ref, 0, 1)):
            for strip in range(0, row_tiles * count, 2):
                strips = range(strip, min(strip + 2, row_tiles * count))
                block = [jnp.concatenate([block_ref[s, c, n] for n in strips], 1) for c in range(column_tiles)]
                product = jnp.dot(lined, jnp.concatenate(block, 0), preferred_element_type=jnp.float32)
                for i, n in enumerate(strips):
                    t = n // count
                    at = t % kept_tiles * operators + first + n % count
                    outs[t // kept_tiles][s, at] = product[:, i * tile : (i + 1) * tile]


def tile_products(vectors, h_block, j_block, layout):
    column_tiles, row_tiles, group, halves, stride, pieces, bits = layout
    sectors, count_vectors = vectors[0].shape[:2]
    count = row_tiles // halves * (J_OPERATORS + 1)
    vmem = pl.BlockSpec(memory_space=pltpu.VMEM)
    shape = jax.ShapeDtypeStruct((sectors, count, count_vectors, h_block.shape[-1]), jnp.float32)
    return pl.pallas_call(
        functools.partial(product_kernel, layout),
        out_shape=[shape] * halves,
        in_specs=[vmem] * (pieces + 2),
        out_specs=[vmem] * halves,
        compiler_params=pltpu.CompilerParams(vmem_limit_bytes=4 << 20),
        name="tile_products",
    )(*vectors, h_block, j_block)


def gram_kernel(x_ref, out_ref):
    sectors, count, vectors, _ = x_ref.shape
    operators = J_OPERATORS + 1
    out_ref[...] = jnp.zeros_like(out_ref)
    for s in range(sectors):
        part = None
        for t in range(count // operators):
            strip = x_ref[s, t * operators : (t + 1) * operators]
            term = lax.dot_general(
                strip[0],
                strip.reshape(operators * vectors, -1),
                (((1,), (1,)), ((), ())),
                precision=exact_precision,
                preferred_element_type=jnp.float32,
            )
            part = term if part is None else part + term
        out_ref[s, :, : operators * vectors] = part


def gram_parts(x):
    sectors, _, vectors, _ = x.shape
    vmem = pl.BlockSpec(memory_space=pltpu.VMEM)
    return pl.pallas_call(
        gram_kernel,
        out_shape=jax.ShapeDtypeStruct((sectors, vectors, LANES), jnp.float32),
        in_specs=[vmem],
        out_specs=vmem,
        compiler_params=pltpu.CompilerParams(vmem_limit_bytes=4 << 20),
        name="gram_parts",
    )(x)


def columns_of(matrix, first, count, width):
    return [jnp.broadcast_to(matrix[:, k : k + 1], (count, width)) for k in range(first, first + count)]


def product_of(columns, right):
    parts = [column * right[k : k + 1, :] for k, column in enumerate(columns)]
    while len(parts) > 1:
        parts = [functools.reduce(jnp.add, parts[i : i + 2]) for i in range(0, len(parts), 2)]
    return parts[0]


def root_kernel(layout, gram_ref, x_ref, basis_ref, elements_ref):
    total_rows, own_tiles, piece, group, halves = layout
    first = lax.axis_index("col") * piece // x_ref.shape[-1]
    own = first if halves == 1 else first // (group * halves) * group + first % group
    vectors, tile = x_ref.shape[2:]
    operators = J_OPERATORS + 1
    shape = (vectors, LANES)
    lanes = lax.broadcasted_iota(jnp.int32, shape, 1)
    is_gram = lanes < vectors
    ranks = lax.broadcasted_iota(jnp.int32, (vectors, 1), 0)
    steps = [jnp.where(ranks == k, 1.5, 0.0).astype(jnp.float32) for k in range(vectors)]
    for s in range(x_ref.shape[0]):
        held = gram_ref[s]
        columns = columns_of(held, 0, vectors, LANES)
        squares = jnp.where(is_gram, held * held, 0.0)
        squares = jnp.sum(jnp.sum(squares, axis=0, keepdims=True), axis=1, keepdims=True)
        scale = jnp.sqrt(squares + 1e-06)
        held = jnp.where(is_gram, held / scale, held)
        blocks = [x_ref[s, (own + t) * operators] for t in range(own_tiles)]
        half = 0.5 / scale
        for iteration in range(NSIT):
            middle = [step - half * column for step, column in zip(steps, columns)]
            once = product_of(middle, held)
            blocks = [product_of(middle, block) for block in blocks]
            if iteration < NSIT - 1:
                held = jnp.where(is_gram, product_of(middle, once), once)
                columns, half = columns_of(held, 0, vectors, LANES), 0.5
            else:
                held = once
        factor = jnp.sqrt(total_rows / scale)
        for t, block in enumerate(blocks):
            basis_ref[s, :, t * tile : (t + 1) * tile] = block * factor
        held = held * (factor / math.sqrt(total_rows))
        for a in range(J_OPERATORS):
            elements_ref[s, a] = held[:, (a + 1) * vectors : (a + 2) * vectors]


def orthonormal(gram, x, layout):
    sectors, _, vectors, tile = x.shape
    vmem = pl.BlockSpec(memory_space=pltpu.VMEM)
    return pl.pallas_call(
        functools.partial(root_kernel, layout),
        out_shape=[
            jax.ShapeDtypeStruct((sectors, vectors, layout[1] * tile), jnp.float32),
            jax.ShapeDtypeStruct((sectors, J_OPERATORS, vectors, vectors), jnp.float32),
        ],
        in_specs=[vmem, vmem],
        out_specs=[vmem, vmem],
        compiler_params=pltpu.CompilerParams(vmem_limit_bytes=4 << 20),
        name="orthonormal",
    )(gram, x)


def per_device(vectors, h_tiles, h_list, j_tiles, j_list):
    sectors, _, piece = vectors.shape
    tile = h_tiles.shape[-1]
    n_row, n_col = lax.axis_size("row"), lax.axis_size("col")
    column = lax.axis_index("col")
    block_rows = piece * n_col
    row_tiles = block_rows // tile
    column_tiles = piece * n_row // tile
    total_rows = block_rows * n_row
    digit = scatter_digit(n_col, piece, tile)
    halves = 1 if digit is None else 2
    group = 1 if digit is None else piece * digit[0] // tile
    stride = 1 if digit is None else digit[0]
    direct = piece == tile and n_row in (2, 4)

    if direct:
        parts = [vectors]
        for mask in range(1, n_row):
            parts.append(lax.ppermute(vectors, "row", [(i, i ^ mask) for i in range(n_row)]))
    else:
        parts = [lax.all_gather(vectors, "row", axis=2, tiled=True)]
    bits = (column_tiles - 1).bit_length()
    layout = (column_tiles, row_tiles, group, halves, stride, len(parts), bits)
    where = spots(h_list.reshape(sectors, -1), j_list.reshape(sectors, -1), layout)
    h_block, j_block = turned(
        where, h_tiles.reshape(sectors, -1, tile, tile), j_tiles.reshape(sectors, -1, tile, tile), layout
    )
    outs = tile_products(parts, h_block, j_block, layout)
    x = outs[0]
    if digit is not None:
        x = x + sent(outs[1], "col", digit, 1)
    for other in digits_of(n_col):
        if other != digit:
            x = summed(x, "col", other)

    gram = gram_parts(x)
    if direct and n_row == 4 and digit is not None:
        gram = gram + across(gram, 1, 0) + across(gram, 2, 0) + across(gram, 3, 0)
        gram = gram + across(gram, 0, digit[0])
    else:
        for other in digits_of(n_row):
            gram = summed(gram, "row", other)
        if digit is not None:
            gram = summed(gram, "col", digit)

    own_tiles = max(1, piece // tile)
    basis, elements = orthonormal(gram, x, (total_rows, own_tiles, piece, group, halves))
    if piece < tile:
        basis = lax.dynamic_slice_in_dim(basis, column * piece % tile, piece, 2)
    return (basis, elements)


def solution(mesh):
    return jax.shard_map(
        per_device,
        mesh=mesh,
        in_specs=(
            P(None, None, ("col", "row")),
            P(None, "row", "col", None, None),
            P(None, "row", "col"),
            P(None, "row", "col", None, None),
            P(None, "row", "col"),
        ),
        out_specs=(P(None, None, ("row", "col")), P()),
        check_vma=False,
    )
```

```python
import functools
import math

import jax
import jax.numpy as jnp
from jax import lax
from jax.experimental import pallas as pl
from jax.experimental.pallas import tpu as pltpu
from jax.sharding import PartitionSpec as P

NSIT = 6
J_OPERATORS = 2
LANES = 128
COVER_FLOPS = 4 << 30

exact_precision = lax.Precision.HIGHEST


def digits_of(size):
    digits, stride = [], 1
    while stride < size:
        rest = size // stride
        factor = next(f for f in range(2, rest + 1) if rest % f == 0)
        digits.append((stride, factor))
        stride *= factor
    return digits


def moved(index, digit, shift):
    stride, factor = digit
    value = index // stride % factor
    return index + ((value + shift) % factor - value) * stride


def sent(x, axis, digit, shift):
    size = lax.axis_size(axis)
    return lax.ppermute(x, axis, [(i, moved(i, digit, shift)) for i in range(size)])


def across(x, row_mask, column_mask):
    n_row, n_col = lax.axis_size("row"), lax.axis_size("col")
    pairs = [(r, c) for r in range(n_row) for c in range(n_col)]
    moves = [(r * n_col + c, (r ^ row_mask) * n_col + (c ^ column_mask)) for r, c in pairs]
    return lax.ppermute(x, ("row", "col"), moves)


def summed(x, axis, digit):
    parts = [sent(x, axis, digit, shift) for shift in range(1, digit[1])]
    return functools.reduce(jnp.add, parts, x)


def scatter_digit(size, piece, tile):
    for stride, factor in digits_of(size):
        if factor == 2 and piece * stride % tile == 0:
            return (stride, factor)
    return None


def quotient(x, divisor, limit):
    if divisor & (divisor - 1) == 0:
        return lax.shift_right_logical(x, divisor.bit_length() - 1)
    marks = range(divisor, limit, divisor)
    return sum((jnp.where(x >= mark, 1, 0) for mark in marks), jnp.zeros_like(x))


def lead_kernel(place_ref):
    place_ref[...] = jnp.full(place_ref.shape, lax.axis_index("row"), jnp.int32)


def spot_kernel(layout, lead_ref, h_list_ref, j_list_ref, spot_ref):
    column_tiles, row_tiles, group, halves, stride, pieces, bits = layout
    positions = row_tiles * column_tiles
    place = lax.axis_index("col") // stride % halves
    turn = lead_ref[:1, :1]
    start = 0
    for list_ref, count in ((h_list_ref, 1), (j_list_ref, J_OPERATORS)):
        code = list_ref[...]
        spot = jnp.maximum(code, 0)
        strip = quotient(spot, column_tiles, J_OPERATORS * positions)
        column = spot - strip * column_tiles
        if pieces > 1:
            column = column ^ turn
        operator = quotient(strip, row_tiles, J_OPERATORS * row_tiles)
        row = strip - operator * row_tiles
        chunk = quotient(row, group, row_tiles)
        outer = quotient(chunk, halves, row_tiles)
        local = outer * group + row - chunk * group
        strips = jnp.where(chunk - outer * halves == place, 0, row_tiles // halves) + local
        at = jnp.where(code >= 0, strips * count + operator, row_tiles * count)
        slots = code.shape[1]
        spot_ref[:, start : start + slots] = lax.shift_left(at, bits) + column
        start += slots


def spots(h_list, j_list, layout):
    vmem = pl.BlockSpec(memory_space=pltpu.VMEM)
    cover = pl.CostEstimate(flops=COVER_FLOPS, transcendentals=0, bytes_accessed=1 << 12)
    lead = pl.pallas_call(
        lead_kernel,
        out_shape=jax.ShapeDtypeStruct((8, LANES), jnp.int32),
        out_specs=vmem,
        compiler_params=pltpu.CompilerParams(vmem_limit_bytes=1 << 20),
        cost_estimate=cover,
        name="lead",
    )()
    return pl.pallas_call(
        functools.partial(spot_kernel, layout),
        out_shape=jax.ShapeDtypeStruct((h_list.shape[0], h_list.shape[1] + j_list.shape[1]), jnp.int32),
        in_specs=[vmem] * 3,
        out_specs=vmem,
        compiler_params=pltpu.CompilerParams(vmem_limit_bytes=1 << 20),
        cost_estimate=cover,
        name="spots",
    )(lead, h_list, j_list)


def turn_kernel(layout, where_ref, h_ref, j_ref, h_block_ref, j_block_ref, spot, arrived):
    bits = layout[-1]
    fetch = pltpu.make_async_copy(where_ref, spot, arrived)
    fetch.start()
    h_block_ref[...] = jnp.zeros_like(h_block_ref)
    j_block_ref[...] = jnp.zeros_like(j_block_ref)
    fetch.wait()
    sectors, h_slots = h_ref.shape[:2]
    for s in range(sectors):
        for tiles, block, first in ((h_ref, h_block_ref, 0), (j_ref, j_block_ref, h_slots)):
            for q in range(tiles.shape[1]):
                word = spot[s, first + q]
                strip = lax.shift_right_logical(word, bits)
                block[s, word & ((1 << bits) - 1), strip] = tiles[s, q].T


def turned(where, h_tiles, j_tiles, layout):
    column_tiles, row_tiles = layout[:2]
    sectors, _, tile, _ = h_tiles.shape
    vmem = pl.BlockSpec(memory_space=pltpu.VMEM)
    shapes = [(sectors, column_tiles, row_tiles * n + 1, tile, tile) for n in (1, J_OPERATORS)]
    moved_bytes = 4 * (h_tiles.size + j_tiles.size)
    return pl.pallas_call(
        functools.partial(turn_kernel, layout),
        out_shape=[jax.ShapeDtypeStruct(shape, h_tiles.dtype) for shape in shapes],
        in_specs=[pl.BlockSpec(memory_space=pl.ANY), vmem, vmem],
        out_specs=[vmem, vmem],
        scratch_shapes=[pltpu.SMEM(where.shape, jnp.int32), pltpu.SemaphoreType.DMA],
        compiler_params=pltpu.CompilerParams(vmem_limit_bytes=4 << 20),
        cost_estimate=pl.CostEstimate(flops=0, transcendentals=0, bytes_accessed=moved_bytes),
        name="turned",
    )(where, h_tiles, j_tiles)


def product_kernel(layout, half, *refs):
    column_tiles, row_tiles, group, halves, stride, pieces, bits = layout
    vector_refs, (h_block_ref, j_block_ref, out_ref) = refs[:pieces], refs[pieces:]
    kept_tiles, operators = row_tiles // halves, J_OPERATORS + 1
    tile = h_block_ref.shape[-1]
    each = column_tiles // pieces
    for s in range(out_ref.shape[0]):
        lined = jnp.concatenate(
            [vector_ref[s, :, t * tile : (t + 1) * tile] for vector_ref in vector_refs for t in range(each)], 1
        )
        for block_ref, first, count in ((j_block_ref, 1, J_OPERATORS), (h_block_ref, 0, 1)):
            start, stop = half * kept_tiles * count, (half + 1) * kept_tiles * count
            for strip in range(start, stop, 2):
                strips = range(strip, min(strip + 2, stop))
                block = [jnp.concatenate([block_ref[s, c, n] for n in strips], 1) for c in range(column_tiles)]
                product = jnp.dot(lined, jnp.concatenate(block, 0), preferred_element_type=jnp.float32)
                for i, n in enumerate(strips):
                    at = n // count % kept_tiles * operators + first + n % count
                    out_ref[s, at] = product[:, i * tile : (i + 1) * tile]


def tile_products(vectors, h_block, j_block, layout, half):
    column_tiles, row_tiles, group, halves, stride, pieces, bits = layout
    sectors, count_vectors = vectors[0].shape[:2]
    tile = h_block.shape[-1]
    count = row_tiles // halves * (J_OPERATORS + 1)
    vmem = pl.BlockSpec(memory_space=pltpu.VMEM)
    return pl.pallas_call(
        functools.partial(product_kernel, layout, half),
        out_shape=jax.ShapeDtypeStruct((sectors, count, count_vectors, tile), jnp.float32),
        in_specs=[vmem] * (pieces + 2),
        out_specs=vmem,
        compiler_params=pltpu.CompilerParams(vmem_limit_bytes=4 << 20),
        cost_estimate=pl.CostEstimate(
            flops=2 * sectors * count * count_vectors * tile * tile * column_tiles,
            transcendentals=0,
            bytes_accessed=2 * sectors * count * tile * tile * column_tiles,
        ),
        name="tile_products",
    )(*vectors, h_block, j_block)


def gram_kernel(x_ref, out_ref):
    sectors, count, vectors, _ = x_ref.shape
    operators = J_OPERATORS + 1
    out_ref[...] = jnp.zeros_like(out_ref)
    for s in range(sectors):
        part = None
        for t in range(count // operators):
            strip = x_ref[s, t * operators : (t + 1) * operators]
            term = lax.dot_general(
                strip[0],
                strip.reshape(operators * vectors, -1),
                (((1,), (1,)), ((), ())),
                precision=exact_precision,
                preferred_element_type=jnp.float32,
            )
            part = term if part is None else part + term
        out_ref[s, :, : operators * vectors] = part


def gram_parts(x):
    sectors, _, vectors, _ = x.shape
    vmem = pl.BlockSpec(memory_space=pltpu.VMEM)
    return pl.pallas_call(
        gram_kernel,
        out_shape=jax.ShapeDtypeStruct((sectors, vectors, LANES), jnp.float32),
        in_specs=[vmem],
        out_specs=vmem,
        compiler_params=pltpu.CompilerParams(vmem_limit_bytes=4 << 20),
        name="gram_parts",
    )(x)


def columns_of(matrix, first, count, width):
    return [jnp.broadcast_to(matrix[:, k : k + 1], (count, width)) for k in range(first, first + count)]


def product_of(columns, right):
    parts = [column * right[k : k + 1, :] for k, column in enumerate(columns)]
    while len(parts) > 1:
        parts = [functools.reduce(jnp.add, parts[i : i + 2]) for i in range(0, len(parts), 2)]
    return parts[0]


def root_kernel(layout, gram_ref, x_ref, basis_ref, elements_ref):
    total_rows, own_tiles, piece, group, halves = layout
    first = lax.axis_index("col") * piece // x_ref.shape[-1]
    own = first if halves == 1 else first // (group * halves) * group + first % group
    vectors, tile = x_ref.shape[2:]
    operators = J_OPERATORS + 1
    shape = (vectors, LANES)
    lanes = lax.broadcasted_iota(jnp.int32, shape, 1)
    is_gram = lanes < vectors
    ranks = lax.broadcasted_iota(jnp.int32, (vectors, 1), 0)
    steps = [jnp.where(ranks == k, 1.5, 0.0).astype(jnp.float32) for k in range(vectors)]
    for s in range(x_ref.shape[0]):
        held = gram_ref[s]
        columns = columns_of(held, 0, vectors, LANES)
        squares = jnp.where(is_gram, held * held, 0.0)
        squares = jnp.sum(jnp.sum(squares, axis=0, keepdims=True), axis=1, keepdims=True)
        scale = jnp.sqrt(squares + 1e-06)
        held = jnp.where(is_gram, held / scale, held)
        blocks = [x_ref[s, (own + t) * operators] for t in range(own_tiles)]
        half = 0.5 / scale
        for iteration in range(NSIT):
            middle = [step - half * column for step, column in zip(steps, columns)]
            once = product_of(middle, held)
            blocks = [product_of(middle, block) for block in blocks]
            if iteration < NSIT - 1:
                held = jnp.where(is_gram, product_of(middle, once), once)
                columns, half = columns_of(held, 0, vectors, LANES), 0.5
            else:
                held = once
        factor = jnp.sqrt(total_rows / scale)
        for t, block in enumerate(blocks):
            basis_ref[s, :, t * tile : (t + 1) * tile] = block * factor
        held = held * (factor / math.sqrt(total_rows))
        for a in range(J_OPERATORS):
            elements_ref[s, a] = held[:, (a + 1) * vectors : (a + 2) * vectors]


def orthonormal(gram, x, layout):
    sectors, _, vectors, tile = x.shape
    vmem = pl.BlockSpec(memory_space=pltpu.VMEM)
    return pl.pallas_call(
        functools.partial(root_kernel, layout),
        out_shape=[
            jax.ShapeDtypeStruct((sectors, vectors, layout[1] * tile), jnp.float32),
            jax.ShapeDtypeStruct((sectors, J_OPERATORS, vectors, vectors), jnp.float32),
        ],
        in_specs=[vmem, vmem],
        out_specs=[vmem, vmem],
        compiler_params=pltpu.CompilerParams(vmem_limit_bytes=4 << 20),
        name="orthonormal",
    )(gram, x)


def per_device(vectors, h_tiles, h_list, j_tiles, j_list):
    sectors, _, piece = vectors.shape
    tile = h_tiles.shape[-1]
    n_row, n_col = lax.axis_size("row"), lax.axis_size("col")
    column = lax.axis_index("col")
    block_rows = piece * n_col
    row_tiles = block_rows // tile
    column_tiles = piece * n_row // tile
    total_rows = block_rows * n_row
    digit = scatter_digit(n_col, piece, tile)
    halves = 1 if digit is None else 2
    group = 1 if digit is None else piece * digit[0] // tile
    stride = 1 if digit is None else digit[0]
    direct = piece == tile and n_row in (2, 4)

    if direct:
        parts = [vectors]
        for mask in range(1, n_row):
            parts.append(lax.ppermute(vectors, "row", [(i, i ^ mask) for i in range(n_row)]))
    else:
        parts = [lax.all_gather(vectors, "row", axis=2, tiled=True)]
    bits = (column_tiles - 1).bit_length()
    layout = (column_tiles, row_tiles, group, halves, stride, len(parts), bits)
    where = spots(h_list.reshape(sectors, -1), j_list.reshape(sectors, -1), layout)
    h_block, j_block = turned(
        where, h_tiles.reshape(sectors, -1, tile, tile), j_tiles.reshape(sectors, -1, tile, tile), layout
    )
    arriving = None
    if digit is not None:
        arriving = sent(tile_products(parts, h_block, j_block, layout, 1), "col", digit, 1)
    x = tile_products(parts, h_block, j_block, layout, 0)
    if digit is not None:
        x = x + arriving
    for other in digits_of(n_col):
        if other != digit:
            x = summed(x, "col", other)

    gram = gram_parts(x)
    if direct and n_row == 4 and digit is not None:
        gram = gram + across(gram, 1, 0) + across(gram, 2, 0) + across(gram, 3, 0)
        gram = gram + across(gram, 0, digit[0])
    else:
        for other in digits_of(n_row):
            gram = summed(gram, "row", other)
        if digit is not None:
            gram = summed(gram, "col", digit)

    own_tiles = max(1, piece // tile)
    basis, elements = orthonormal(gram, x, (total_rows, own_tiles, piece, group, halves))
    if piece < tile:
        basis = lax.dynamic_slice_in_dim(basis, column * piece % tile, piece, 2)
    return (basis, elements)


def solution(mesh):
    return jax.shard_map(
        per_device,
        mesh=mesh,
        in_specs=(
            P(None, None, ("col", "row")),
            P(None, "row", "col", None, None),
            P(None, "row", "col"),
            P(None, "row", "col", None, None),
            P(None, "row", "col"),
        ),
        out_specs=(P(None, None, ("row", "col")), P()),
        check_vma=False,
    )
```

```python
import functools
import math

import jax
import jax.numpy as jnp
from jax import lax
from jax.experimental import pallas as pl
from jax.experimental.pallas import tpu as pltpu
from jax.sharding import PartitionSpec as P

NSIT = 6
J_OPERATORS = 2
LANES = 128
COVER_FLOPS = 4 << 30

exact_precision = lax.Precision.HIGHEST


def digits_of(size):
    digits, stride = [], 1
    while stride < size:
        rest = size // stride
        factor = next(f for f in range(2, rest + 1) if rest % f == 0)
        digits.append((stride, factor))
        stride *= factor
    return digits


def moved(index, digit, shift):
    stride, factor = digit
    value = index // stride % factor
    return index + ((value + shift) % factor - value) * stride


def sent(x, axis, digit, shift):
    size = lax.axis_size(axis)
    return lax.ppermute(x, axis, [(i, moved(i, digit, shift)) for i in range(size)])


def across(x, row_mask, column_mask):
    n_row, n_col = lax.axis_size("row"), lax.axis_size("col")
    pairs = [(r, c) for r in range(n_row) for c in range(n_col)]
    moves = [(r * n_col + c, (r ^ row_mask) * n_col + (c ^ column_mask)) for r, c in pairs]
    return lax.ppermute(x, ("row", "col"), moves)


def summed(x, axis, digit):
    parts = [sent(x, axis, digit, shift) for shift in range(1, digit[1])]
    return functools.reduce(jnp.add, parts, x)


def scatter_digit(size, piece, tile):
    for stride, factor in digits_of(size):
        if factor == 2 and piece * stride % tile == 0:
            return (stride, factor)
    return None


def quotient(x, divisor, limit):
    if divisor & (divisor - 1) == 0:
        return lax.shift_right_logical(x, divisor.bit_length() - 1)
    marks = range(divisor, limit, divisor)
    return sum((jnp.where(x >= mark, 1, 0) for mark in marks), jnp.zeros_like(x))


def lead_kernel(place_ref):
    place_ref[...] = jnp.full(place_ref.shape, lax.axis_index("row"), jnp.int32)


def spot_kernel(layout, lead_ref, h_list_ref, j_list_ref, spot_ref):
    column_tiles, row_tiles, group, halves, stride, pieces, bits = layout
    positions = row_tiles * column_tiles
    place = lax.axis_index("col") // stride % halves
    turn = lead_ref[:1, :1]
    start = 0
    for list_ref, count in ((h_list_ref, 1), (j_list_ref, J_OPERATORS)):
        code = list_ref[...]
        spot = jnp.maximum(code, 0)
        strip = quotient(spot, column_tiles, J_OPERATORS * positions)
        column = spot - strip * column_tiles
        if pieces > 1:
            column = column ^ turn
        operator = quotient(strip, row_tiles, J_OPERATORS * row_tiles)
        row = strip - operator * row_tiles
        chunk = quotient(row, group, row_tiles)
        outer = quotient(chunk, halves, row_tiles)
        local = outer * group + row - chunk * group
        strips = jnp.where(chunk - outer * halves == place, 0, row_tiles // halves) + local
        at = jnp.where(code >= 0, strips * count + operator, row_tiles * count)
        slots = code.shape[1]
        spot_ref[:, start : start + slots] = lax.shift_left(at, bits) + column
        start += slots


def spots(h_list, j_list, layout):
    vmem = pl.BlockSpec(memory_space=pltpu.VMEM)
    cover = pl.CostEstimate(flops=COVER_FLOPS, transcendentals=0, bytes_accessed=1 << 12)
    lead = pl.pallas_call(
        lead_kernel,
        out_shape=jax.ShapeDtypeStruct((8, LANES), jnp.int32),
        out_specs=vmem,
        compiler_params=pltpu.CompilerParams(vmem_limit_bytes=1 << 20),
        cost_estimate=cover,
        name="lead",
    )()
    return pl.pallas_call(
        functools.partial(spot_kernel, layout),
        out_shape=jax.ShapeDtypeStruct((h_list.shape[0], h_list.shape[1] + j_list.shape[1]), jnp.int32),
        in_specs=[vmem] * 3,
        out_specs=vmem,
        compiler_params=pltpu.CompilerParams(vmem_limit_bytes=1 << 20),
        cost_estimate=cover,
        name="spots",
    )(lead, h_list, j_list)


def turn_kernel(layout, where_ref, h_ref, j_ref, h_block_ref, j_block_ref, spot, arrived):
    bits = layout[-1]
    fetch = pltpu.make_async_copy(where_ref, spot, arrived)
    fetch.start()
    h_block_ref[...] = jnp.zeros_like(h_block_ref)
    j_block_ref[...] = jnp.zeros_like(j_block_ref)
    fetch.wait()
    sectors, h_slots = h_ref.shape[:2]
    for s in range(sectors):
        for tiles, block, first in ((h_ref, h_block_ref, 0), (j_ref, j_block_ref, h_slots)):
            for q in range(tiles.shape[1]):
                word = spot[s, first + q]
                strip = lax.shift_right_logical(word, bits)
                block[s, word & ((1 << bits) - 1), strip] = tiles[s, q].T


def turned(where, h_tiles, j_tiles, layout):
    column_tiles, row_tiles = layout[:2]
    sectors, _, tile, _ = h_tiles.shape
    vmem = pl.BlockSpec(memory_space=pltpu.VMEM)
    shapes = [(sectors, column_tiles, row_tiles * n + 1, tile, tile) for n in (1, J_OPERATORS)]
    moved_bytes = 4 * (h_tiles.size + j_tiles.size)
    return pl.pallas_call(
        functools.partial(turn_kernel, layout),
        out_shape=[jax.ShapeDtypeStruct(shape, h_tiles.dtype) for shape in shapes],
        in_specs=[pl.BlockSpec(memory_space=pl.ANY), vmem, vmem],
        out_specs=[vmem, vmem],
        scratch_shapes=[pltpu.SMEM(where.shape, jnp.int32), pltpu.SemaphoreType.DMA],
        compiler_params=pltpu.CompilerParams(vmem_limit_bytes=4 << 20),
        cost_estimate=pl.CostEstimate(flops=0, transcendentals=0, bytes_accessed=moved_bytes),
        name="turned",
    )(where, h_tiles, j_tiles)


def product_kernel(layout, half, *refs):
    column_tiles, row_tiles, group, halves, stride, pieces, bits = layout
    vector_refs, (h_block_ref, j_block_ref, out_ref) = refs[:pieces], refs[pieces:]
    kept_tiles, operators = row_tiles // halves, J_OPERATORS + 1
    tile = h_block_ref.shape[-1]
    each = column_tiles // pieces
    for s in range(out_ref.shape[0]):
        lined = jnp.concatenate(
            [vector_ref[s, :, t * tile : (t + 1) * tile] for vector_ref in vector_refs for t in range(each)], 1
        )
        for block_ref, first, count in ((j_block_ref, 1, J_OPERATORS), (h_block_ref, 0, 1)):
            start, stop = half * kept_tiles * count, (half + 1) * kept_tiles * count
            for strip in range(start, stop, 2):
                strips = range(strip, min(strip + 2, stop))
                block = [jnp.concatenate([block_ref[s, c, n] for n in strips], 1) for c in range(column_tiles)]
                product = jnp.dot(lined, jnp.concatenate(block, 0), preferred_element_type=jnp.float32)
                for i, n in enumerate(strips):
                    at = n // count % kept_tiles * operators + first + n % count
                    out_ref[s, at] = product[:, i * tile : (i + 1) * tile]


def tile_products(vectors, h_block, j_block, layout, half):
    column_tiles, row_tiles, group, halves, stride, pieces, bits = layout
    sectors, count_vectors = vectors[0].shape[:2]
    tile = h_block.shape[-1]
    count = row_tiles // halves * (J_OPERATORS + 1)
    vmem = pl.BlockSpec(memory_space=pltpu.VMEM)
    return pl.pallas_call(
        functools.partial(product_kernel, layout, half),
        out_shape=jax.ShapeDtypeStruct((sectors, count, count_vectors, tile), jnp.float32),
        in_specs=[vmem] * (pieces + 2),
        out_specs=vmem,
        compiler_params=pltpu.CompilerParams(vmem_limit_bytes=4 << 20),
        cost_estimate=pl.CostEstimate(
            flops=2 * sectors * count * count_vectors * tile * tile * column_tiles,
            transcendentals=0,
            bytes_accessed=2 * sectors * count * tile * tile * column_tiles,
        ),
        name="tile_products",
    )(*vectors, h_block, j_block)


def gram_kernel(x_ref, out_ref):
    sectors, count, vectors, _ = x_ref.shape
    operators = J_OPERATORS + 1
    out_ref[...] = jnp.zeros_like(out_ref)
    for s in range(sectors):
        strips = [x_ref[s, t * operators : (t + 1) * operators] for t in range(count // operators)]
        right = jnp.concatenate([strip.reshape(operators * vectors, -1) for strip in strips], 1)
        out_ref[s, :, : operators * vectors] = lax.dot_general(
            right[:vectors],
            right,
            (((1,), (1,)), ((), ())),
            precision=exact_precision,
            preferred_element_type=jnp.float32,
        )


def gram_parts(x):
    sectors, _, vectors, _ = x.shape
    vmem = pl.BlockSpec(memory_space=pltpu.VMEM)
    return pl.pallas_call(
        gram_kernel,
        out_shape=jax.ShapeDtypeStruct((sectors, vectors, LANES), jnp.float32),
        in_specs=[vmem],
        out_specs=vmem,
        compiler_params=pltpu.CompilerParams(vmem_limit_bytes=4 << 20),
        name="gram_parts",
    )(x)


def columns_of(matrix, first, count, width):
    return [jnp.broadcast_to(matrix[:, k : k + 1], (count, width)) for k in range(first, first + count)]


def product_of(columns, right):
    parts = [column * right[k : k + 1, :] for k, column in enumerate(columns)]
    while len(parts) > 1:
        parts = [functools.reduce(jnp.add, parts[i : i + 2]) for i in range(0, len(parts), 2)]
    return parts[0]


def root_kernel(layout, gram_ref, x_ref, basis_ref, elements_ref):
    total_rows, own_tiles, piece, group, halves = layout
    first = lax.axis_index("col") * piece // x_ref.shape[-1]
    own = first if halves == 1 else first // (group * halves) * group + first % group
    vectors, tile = x_ref.shape[2:]
    operators = J_OPERATORS + 1
    shape = (vectors, LANES)
    lanes = lax.broadcasted_iota(jnp.int32, shape, 1)
    is_gram = lanes < vectors
    ranks = lax.broadcasted_iota(jnp.int32, (vectors, 1), 0)
    steps = [jnp.where(ranks == k, 1.5, 0.0).astype(jnp.float32) for k in range(vectors)]
    for s in range(x_ref.shape[0]):
        held = gram_ref[s]
        columns = columns_of(held, 0, vectors, LANES)
        squares = jnp.where(is_gram, held * held, 0.0)
        squares = jnp.sum(jnp.sum(squares, axis=0, keepdims=True), axis=1, keepdims=True)
        scale = jnp.sqrt(squares + 1e-06)
        held = jnp.where(is_gram, held / scale, held)
        blocks = [x_ref[s, (own + t) * operators] for t in range(own_tiles)]
        half = 0.5 / scale
        for iteration in range(NSIT):
            middle = [step - half * column for step, column in zip(steps, columns)]
            once = product_of(middle, held)
            blocks = [product_of(middle, block) for block in blocks]
            if iteration < NSIT - 1:
                held = jnp.where(is_gram, product_of(middle, once), once)
                columns, half = columns_of(held, 0, vectors, LANES), 0.5
            else:
                held = once
        factor = jnp.sqrt(total_rows / scale)
        for t, block in enumerate(blocks):
            basis_ref[s, :, t * tile : (t + 1) * tile] = block * factor
        held = held * (factor / math.sqrt(total_rows))
        for a in range(J_OPERATORS):
            elements_ref[s, a] = held[:, (a + 1) * vectors : (a + 2) * vectors]


def orthonormal(gram, x, layout):
    sectors, _, vectors, tile = x.shape
    vmem = pl.BlockSpec(memory_space=pltpu.VMEM)
    return pl.pallas_call(
        functools.partial(root_kernel, layout),
        out_shape=[
            jax.ShapeDtypeStruct((sectors, vectors, layout[1] * tile), jnp.float32),
            jax.ShapeDtypeStruct((sectors, J_OPERATORS, vectors, vectors), jnp.float32),
        ],
        in_specs=[vmem, vmem],
        out_specs=[vmem, vmem],
        compiler_params=pltpu.CompilerParams(vmem_limit_bytes=4 << 20),
        name="orthonormal",
    )(gram, x)


def per_device(vectors, h_tiles, h_list, j_tiles, j_list):
    sectors, _, piece = vectors.shape
    tile = h_tiles.shape[-1]
    n_row, n_col = lax.axis_size("row"), lax.axis_size("col")
    column = lax.axis_index("col")
    block_rows = piece * n_col
    row_tiles = block_rows // tile
    column_tiles = piece * n_row // tile
    total_rows = block_rows * n_row
    digit = scatter_digit(n_col, piece, tile)
    halves = 1 if digit is None else 2
    group = 1 if digit is None else piece * digit[0] // tile
    stride = 1 if digit is None else digit[0]
    direct = piece == tile and n_row in (2, 4)

    if direct:
        parts = [vectors]
        for mask in range(1, n_row):
            parts.append(lax.ppermute(vectors, "row", [(i, i ^ mask) for i in range(n_row)]))
    else:
        parts = [lax.all_gather(vectors, "row", axis=2, tiled=True)]
    bits = (column_tiles - 1).bit_length()
    layout = (column_tiles, row_tiles, group, halves, stride, len(parts), bits)
    where = spots(h_list.reshape(sectors, -1), j_list.reshape(sectors, -1), layout)
    h_block, j_block = turned(
        where, h_tiles.reshape(sectors, -1, tile, tile), j_tiles.reshape(sectors, -1, tile, tile), layout
    )
    arriving = None
    if digit is not None:
        arriving = sent(tile_products(parts, h_block, j_block, layout, 1), "col", digit, 1)
    x = tile_products(parts, h_block, j_block, layout, 0)
    if digit is not None:
        x = x + arriving
    for other in digits_of(n_col):
        if other != digit:
            x = summed(x, "col", other)

    gram = gram_parts(x)
    if direct and n_row == 4 and digit is not None:
        gram = gram + across(gram, 1, 0) + across(gram, 2, 0) + across(gram, 3, 0)
        gram = gram + across(gram, 0, digit[0])
    else:
        for other in digits_of(n_row):
            gram = summed(gram, "row", other)
        if digit is not None:
            gram = summed(gram, "col", digit)

    own_tiles = max(1, piece // tile)
    basis, elements = orthonormal(gram, x, (total_rows, own_tiles, piece, group, halves))
    if piece < tile:
        basis = lax.dynamic_slice_in_dim(basis, column * piece % tile, piece, 2)
    return (basis, elements)


def solution(mesh):
    return jax.shard_map(
        per_device,
        mesh=mesh,
        in_specs=(
            P(None, None, ("col", "row")),
            P(None, "row", "col", None, None),
            P(None, "row", "col"),
            P(None, "row", "col", None, None),
            P(None, "row", "col"),
        ),
        out_specs=(P(None, None, ("row", "col")), P()),
        check_vma=False,
    )
```

```python
import functools
import math

import jax
import jax.numpy as jnp
from jax import lax
from jax.experimental import pallas as pl
from jax.experimental.pallas import tpu as pltpu
from jax.sharding import PartitionSpec as P

NSIT = 6
J_OPERATORS = 2
LANES = 128
COVER_FLOPS = 4 << 30

exact_precision = lax.Precision.HIGHEST


def digits_of(size):
    digits, stride = [], 1
    while stride < size:
        rest = size // stride
        factor = next(f for f in range(2, rest + 1) if rest % f == 0)
        digits.append((stride, factor))
        stride *= factor
    return digits


def moved(index, digit, shift):
    stride, factor = digit
    value = index // stride % factor
    return index + ((value + shift) % factor - value) * stride


def sent(x, axis, digit, shift):
    size = lax.axis_size(axis)
    return lax.ppermute(x, axis, [(i, moved(i, digit, shift)) for i in range(size)])


def across(x, row_mask, column_mask):
    n_row, n_col = lax.axis_size("row"), lax.axis_size("col")
    pairs = [(r, c) for r in range(n_row) for c in range(n_col)]
    moves = [(r * n_col + c, (r ^ row_mask) * n_col + (c ^ column_mask)) for r, c in pairs]
    return lax.ppermute(x, ("row", "col"), moves)


def summed(x, axis, digit):
    parts = [sent(x, axis, digit, shift) for shift in range(1, digit[1])]
    return functools.reduce(jnp.add, parts, x)


def scatter_digit(size, piece, tile):
    for stride, factor in digits_of(size):
        if factor == 2 and stride > 1 and piece * stride % tile == 0:
            return (stride, factor)
    return None


def quotient(x, divisor, limit):
    if divisor & (divisor - 1) == 0:
        return lax.shift_right_logical(x, divisor.bit_length() - 1)
    marks = range(divisor, limit, divisor)
    return sum((jnp.where(x >= mark, 1, 0) for mark in marks), jnp.zeros_like(x))


def lead_kernel(place_ref):
    place_ref[...] = jnp.full(place_ref.shape, lax.axis_index("row"), jnp.int32)


def spot_kernel(layout, lead_ref, h_list_ref, j_list_ref, spot_ref):
    column_tiles, row_tiles, group, halves, stride, pieces, bits = layout
    positions = row_tiles * column_tiles
    place = lax.axis_index("col") // stride % halves
    turn = lead_ref[:1, :1]
    start = 0
    for list_ref, count in ((h_list_ref, 1), (j_list_ref, J_OPERATORS)):
        code = list_ref[...]
        spot = jnp.maximum(code, 0)
        strip = quotient(spot, column_tiles, J_OPERATORS * positions)
        column = spot - strip * column_tiles
        if pieces > 1:
            column = column ^ turn
        operator = quotient(strip, row_tiles, J_OPERATORS * row_tiles)
        row = strip - operator * row_tiles
        chunk = quotient(row, group, row_tiles)
        outer = quotient(chunk, halves, row_tiles)
        local = outer * group + row - chunk * group
        strips = jnp.where(chunk - outer * halves == place, 0, row_tiles // halves) + local
        at = jnp.where(code >= 0, strips * count + operator, row_tiles * count)
        slots = code.shape[1]
        spot_ref[:, start : start + slots] = lax.shift_left(at, bits) + column
        start += slots


def spots(h_list, j_list, layout):
    vmem = pl.BlockSpec(memory_space=pltpu.VMEM)
    cover = pl.CostEstimate(flops=COVER_FLOPS, transcendentals=0, bytes_accessed=1 << 12)
    lead = pl.pallas_call(
        lead_kernel,
        out_shape=jax.ShapeDtypeStruct((8, LANES), jnp.int32),
        out_specs=vmem,
        compiler_params=pltpu.CompilerParams(vmem_limit_bytes=1 << 20),
        cost_estimate=cover,
        name="lead",
    )()
    return pl.pallas_call(
        functools.partial(spot_kernel, layout),
        out_shape=jax.ShapeDtypeStruct((h_list.shape[0], h_list.shape[1] + j_list.shape[1]), jnp.int32),
        in_specs=[vmem] * 3,
        out_specs=vmem,
        compiler_params=pltpu.CompilerParams(vmem_limit_bytes=1 << 20),
        cost_estimate=cover,
        name="spots",
    )(lead, h_list, j_list)


def turn_kernel(layout, where_ref, h_ref, j_ref, h_block_ref, j_block_ref, spot, arrived):
    bits = layout[-1]
    fetch = pltpu.make_async_copy(where_ref, spot, arrived)
    fetch.start()
    h_block_ref[...] = jnp.zeros_like(h_block_ref)
    j_block_ref[...] = jnp.zeros_like(j_block_ref)
    fetch.wait()
    sectors, h_slots = h_ref.shape[:2]
    for s in range(sectors):
        for tiles, block, first in ((h_ref, h_block_ref, 0), (j_ref, j_block_ref, h_slots)):
            for q in range(tiles.shape[1]):
                word = spot[s, first + q]
                strip = lax.shift_right_logical(word, bits)
                block[s, word & ((1 << bits) - 1), strip] = tiles[s, q].T


def turned(where, h_tiles, j_tiles, layout):
    column_tiles, row_tiles = layout[:2]
    sectors, _, tile, _ = h_tiles.shape
    vmem = pl.BlockSpec(memory_space=pltpu.VMEM)
    shapes = [(sectors, column_tiles, row_tiles * n + 1, tile, tile) for n in (1, J_OPERATORS)]
    moved_bytes = 4 * (h_tiles.size + j_tiles.size)
    return pl.pallas_call(
        functools.partial(turn_kernel, layout),
        out_shape=[jax.ShapeDtypeStruct(shape, h_tiles.dtype) for shape in shapes],
        in_specs=[pl.BlockSpec(memory_space=pl.ANY), vmem, vmem],
        out_specs=[vmem, vmem],
        scratch_shapes=[pltpu.SMEM(where.shape, jnp.int32), pltpu.SemaphoreType.DMA],
        compiler_params=pltpu.CompilerParams(vmem_limit_bytes=4 << 20),
        cost_estimate=pl.CostEstimate(flops=0, transcendentals=0, bytes_accessed=moved_bytes),
        name="turned",
    )(where, h_tiles, j_tiles)


def product_kernel(layout, half, *refs):
    column_tiles, row_tiles, group, halves, stride, pieces, bits = layout
    vector_refs, (h_block_ref, j_block_ref, out_ref) = refs[:pieces], refs[pieces:]
    kept_tiles, operators = row_tiles // halves, J_OPERATORS + 1
    tile = h_block_ref.shape[-1]
    each = column_tiles // pieces
    for s in range(out_ref.shape[0]):
        lined = jnp.concatenate(
            [vector_ref[s, :, t * tile : (t + 1) * tile] for vector_ref in vector_refs for t in range(each)], 1
        )
        for block_ref, first, count in ((j_block_ref, 1, J_OPERATORS), (h_block_ref, 0, 1)):
            start, stop = half * kept_tiles * count, (half + 1) * kept_tiles * count
            for strip in range(start, stop, 2):
                strips = range(strip, min(strip + 2, stop))
                block = [jnp.concatenate([block_ref[s, c, n] for n in strips], 1) for c in range(column_tiles)]
                product = jnp.dot(lined, jnp.concatenate(block, 0), preferred_element_type=jnp.float32)
                for i, n in enumerate(strips):
                    at = n // count % kept_tiles * operators + first + n % count
                    out_ref[s, at] = product[:, i * tile : (i + 1) * tile]


def tile_products(vectors, h_block, j_block, layout, half):
    column_tiles, row_tiles, group, halves, stride, pieces, bits = layout
    sectors, count_vectors = vectors[0].shape[:2]
    tile = h_block.shape[-1]
    count = row_tiles // halves * (J_OPERATORS + 1)
    vmem = pl.BlockSpec(memory_space=pltpu.VMEM)
    return pl.pallas_call(
        functools.partial(product_kernel, layout, half),
        out_shape=jax.ShapeDtypeStruct((sectors, count, count_vectors, tile), jnp.float32),
        in_specs=[vmem] * (pieces + 2),
        out_specs=vmem,
        compiler_params=pltpu.CompilerParams(vmem_limit_bytes=4 << 20),
        cost_estimate=pl.CostEstimate(
            flops=2 * sectors * count * count_vectors * tile * tile * column_tiles,
            transcendentals=0,
            bytes_accessed=2 * sectors * count * tile * tile * column_tiles,
        ),
        name="tile_products",
    )(*vectors, h_block, j_block)


def gram_kernel(x_ref, out_ref):
    sectors, count, vectors, _ = x_ref.shape
    operators = J_OPERATORS + 1
    out_ref[...] = jnp.zeros_like(out_ref)
    for s in range(sectors):
        strips = [x_ref[s, t * operators : (t + 1) * operators] for t in range(count // operators)]
        right = jnp.concatenate([strip.reshape(operators * vectors, -1) for strip in strips], 1)
        out_ref[s, :, : operators * vectors] = lax.dot_general(
            right[:vectors],
            right,
            (((1,), (1,)), ((), ())),
            precision=exact_precision,
            preferred_element_type=jnp.float32,
        )


def gram_parts(x):
    sectors, _, vectors, _ = x.shape
    vmem = pl.BlockSpec(memory_space=pltpu.VMEM)
    return pl.pallas_call(
        gram_kernel,
        out_shape=jax.ShapeDtypeStruct((sectors, vectors, LANES), jnp.float32),
        in_specs=[vmem],
        out_specs=vmem,
        compiler_params=pltpu.CompilerParams(vmem_limit_bytes=4 << 20),
        name="gram_parts",
    )(x)


def columns_of(matrix, first, count, width):
    return [jnp.broadcast_to(matrix[:, k : k + 1], (count, width)) for k in range(first, first + count)]


def product_of(columns, right):
    parts = [column * right[k : k + 1, :] for k, column in enumerate(columns)]
    while len(parts) > 1:
        parts = [functools.reduce(jnp.add, parts[i : i + 2]) for i in range(0, len(parts), 2)]
    return parts[0]


def root_kernel(layout, gram_ref, x_ref, basis_ref, elements_ref):
    total_rows, own_tiles, piece, group, halves = layout
    first = lax.axis_index("col") * piece // x_ref.shape[-1]
    own = first if halves == 1 else first // (group * halves) * group + first % group
    vectors, tile = x_ref.shape[2:]
    operators = J_OPERATORS + 1
    shape = (vectors, LANES)
    lanes = lax.broadcasted_iota(jnp.int32, shape, 1)
    is_gram = lanes < vectors
    ranks = lax.broadcasted_iota(jnp.int32, (vectors, 1), 0)
    steps = [jnp.where(ranks == k, 1.5, 0.0).astype(jnp.float32) for k in range(vectors)]
    for s in range(x_ref.shape[0]):
        held = gram_ref[s]
        columns = columns_of(held, 0, vectors, LANES)
        squares = jnp.where(is_gram, held * held, 0.0)
        squares = jnp.sum(jnp.sum(squares, axis=0, keepdims=True), axis=1, keepdims=True)
        scale = jnp.sqrt(squares + 1e-06)
        held = jnp.where(is_gram, held / scale, held)
        blocks = [x_ref[s, (own + t) * operators] for t in range(own_tiles)]
        half = 0.5 / scale
        for iteration in range(NSIT):
            middle = [step - half * column for step, column in zip(steps, columns)]
            once = product_of(middle, held)
            blocks = [product_of(middle, block) for block in blocks]
            if iteration < NSIT - 1:
                held = jnp.where(is_gram, product_of(middle, once), once)
                columns, half = columns_of(held, 0, vectors, LANES), 0.5
            else:
                held = once
        factor = jnp.sqrt(total_rows / scale)
        for t, block in enumerate(blocks):
            basis_ref[s, :, t * tile : (t + 1) * tile] = block * factor
        held = held * (factor / math.sqrt(total_rows))
        for a in range(J_OPERATORS):
            elements_ref[s, a] = held[:, (a + 1) * vectors : (a + 2) * vectors]


def orthonormal(gram, x, layout):
    sectors, _, vectors, tile = x.shape
    vmem = pl.BlockSpec(memory_space=pltpu.VMEM)
    return pl.pallas_call(
        functools.partial(root_kernel, layout),
        out_shape=[
            jax.ShapeDtypeStruct((sectors, vectors, layout[1] * tile), jnp.float32),
            jax.ShapeDtypeStruct((sectors, J_OPERATORS, vectors, vectors), jnp.float32),
        ],
        in_specs=[vmem, vmem],
        out_specs=[vmem, vmem],
        compiler_params=pltpu.CompilerParams(vmem_limit_bytes=4 << 20),
        name="orthonormal",
    )(gram, x)


def per_device(vectors, h_tiles, h_list, j_tiles, j_list):
    sectors, _, piece = vectors.shape
    tile = h_tiles.shape[-1]
    n_row, n_col = lax.axis_size("row"), lax.axis_size("col")
    column = lax.axis_index("col")
    block_rows = piece * n_col
    row_tiles = block_rows // tile
    column_tiles = piece * n_row // tile
    total_rows = block_rows * n_row
    digit = scatter_digit(n_col, piece, tile)
    halves = 1 if digit is None else 2
    group = 1 if digit is None else piece * digit[0] // tile
    stride = 1 if digit is None else digit[0]
    direct = piece == tile and n_row in (2, 4)

    if direct:
        parts = [vectors]
        for mask in range(1, n_row):
            parts.append(lax.ppermute(vectors, "row", [(i, i ^ mask) for i in range(n_row)]))
    else:
        parts = [lax.all_gather(vectors, "row", axis=2, tiled=True)]
    bits = (column_tiles - 1).bit_length()
    layout = (column_tiles, row_tiles, group, halves, stride, len(parts), bits)
    where = spots(h_list.reshape(sectors, -1), j_list.reshape(sectors, -1), layout)
    h_block, j_block = turned(
        where, h_tiles.reshape(sectors, -1, tile, tile), j_tiles.reshape(sectors, -1, tile, tile), layout
    )
    arriving = None
    if digit is not None:
        arriving = sent(tile_products(parts, h_block, j_block, layout, 1), "col", digit, 1)
    x = tile_products(parts, h_block, j_block, layout, 0)
    if digit is not None:
        x = x + arriving
    for other in digits_of(n_col):
        if other != digit:
            x = summed(x, "col", other)

    gram = gram_parts(x)
    if direct and n_row == 4 and digit is not None:
        gram = gram + across(gram, 0, digit[0])
        gram = gram + across(gram, 1, 0) + across(gram, 2, 0) + across(gram, 3, 0)
    else:
        for other in digits_of(n_row):
            gram = summed(gram, "row", other)
        if digit is not None:
            gram = summed(gram, "col", digit)

    own_tiles = max(1, piece // tile)
    basis, elements = orthonormal(gram, x, (total_rows, own_tiles, piece, group, halves))
    if piece < tile:
        basis = lax.dynamic_slice_in_dim(basis, column * piece % tile, piece, 2)
    return (basis, elements)


def solution(mesh):
    return jax.shard_map(
        per_device,
        mesh=mesh,
        in_specs=(
            P(None, None, ("col", "row")),
            P(None, "row", "col", None, None),
            P(None, "row", "col"),
            P(None, "row", "col", None, None),
            P(None, "row", "col"),
        ),
        out_specs=(P(None, None, ("row", "col")), P()),
        check_vma=False,
    )
```

```python
import functools
import math

import jax
import jax.numpy as jnp
from jax import lax
from jax.experimental import pallas as pl
from jax.experimental.pallas import tpu as pltpu
from jax.sharding import PartitionSpec as P

NSIT = 6
J_OPERATORS = 2
LANES = 128
COVER_FLOPS = 4 << 30

exact_precision = lax.Precision.HIGHEST


def digits_of(size):
    digits, stride = [], 1
    while stride < size:
        rest = size // stride
        factor = next(f for f in range(2, rest + 1) if rest % f == 0)
        digits.append((stride, factor))
        stride *= factor
    return digits


def moved(index, digit, shift):
    stride, factor = digit
    value = index // stride % factor
    return index + ((value + shift) % factor - value) * stride


def sent(x, axis, digit, shift):
    size = lax.axis_size(axis)
    return lax.ppermute(x, axis, [(i, moved(i, digit, shift)) for i in range(size)])


def across(x, row_mask, column_mask):
    n_row, n_col = lax.axis_size("row"), lax.axis_size("col")
    pairs = [(r, c) for r in range(n_row) for c in range(n_col)]
    moves = [(r * n_col + c, (r ^ row_mask) * n_col + (c ^ column_mask)) for r, c in pairs]
    return lax.ppermute(x, ("row", "col"), moves)


def summed(x, axis, digit):
    parts = [sent(x, axis, digit, shift) for shift in range(1, digit[1])]
    return functools.reduce(jnp.add, parts, x)


def scatter_digit(size, piece, tile):
    for stride, factor in digits_of(size):
        if factor == 2 and piece * stride % tile == 0:
            return (stride, factor)
    return None


def quotient(x, divisor, limit):
    if divisor & (divisor - 1) == 0:
        return lax.shift_right_logical(x, divisor.bit_length() - 1)
    marks = range(divisor, limit, divisor)
    return sum((jnp.where(x >= mark, 1, 0) for mark in marks), jnp.zeros_like(x))


def lead_kernel(place_ref):
    place_ref[...] = jnp.full(place_ref.shape, lax.axis_index("row"), jnp.int32)


def spot_kernel(layout, lead_ref, h_list_ref, j_list_ref, spot_ref):
    column_tiles, row_tiles, group, halves, stride, pieces, bits = layout
    positions = row_tiles * column_tiles
    place = lax.axis_index("col") // stride % halves
    turn = lead_ref[:1, :1]
    start = 0
    for list_ref, count in ((h_list_ref, 1), (j_list_ref, J_OPERATORS)):
        code = list_ref[...]
        spot = jnp.maximum(code, 0)
        strip = quotient(spot, column_tiles, J_OPERATORS * positions)
        column = spot - strip * column_tiles
        if pieces > 1:
            column = column ^ turn
        operator = quotient(strip, row_tiles, J_OPERATORS * row_tiles)
        row = strip - operator * row_tiles
        chunk = quotient(row, group, row_tiles)
        outer = quotient(chunk, halves, row_tiles)
        local = outer * group + row - chunk * group
        strips = jnp.where(chunk - outer * halves == place, 0, row_tiles // halves) + local
        at = jnp.where(code >= 0, strips * count + operator, row_tiles * count)
        slots = code.shape[1]
        spot_ref[:, start : start + slots] = lax.shift_left(at, bits) + column
        start += slots


def spots(h_list, j_list, layout):
    vmem = pl.BlockSpec(memory_space=pltpu.VMEM)
    cover = pl.CostEstimate(flops=COVER_FLOPS, transcendentals=0, bytes_accessed=1 << 12)
    lead = pl.pallas_call(
        lead_kernel,
        out_shape=jax.ShapeDtypeStruct((8, LANES), jnp.int32),
        out_specs=vmem,
        compiler_params=pltpu.CompilerParams(vmem_limit_bytes=1 << 20),
        cost_estimate=cover,
        name="lead",
    )()
    return pl.pallas_call(
        functools.partial(spot_kernel, layout),
        out_shape=jax.ShapeDtypeStruct((h_list.shape[0], h_list.shape[1] + j_list.shape[1]), jnp.int32),
        in_specs=[vmem] * 3,
        out_specs=vmem,
        compiler_params=pltpu.CompilerParams(vmem_limit_bytes=1 << 20),
        cost_estimate=cover,
        name="spots",
    )(lead, h_list, j_list)


def turn_kernel(layout, where_ref, h_ref, j_ref, h_block_ref, j_block_ref, spot, arrived):
    bits = layout[-1]
    fetch = pltpu.make_async_copy(where_ref, spot, arrived)
    fetch.start()
    h_block_ref[...] = jnp.zeros_like(h_block_ref)
    j_block_ref[...] = jnp.zeros_like(j_block_ref)
    fetch.wait()
    sectors, h_slots = h_ref.shape[:2]
    for s in range(sectors):
        for tiles, block, first in ((h_ref, h_block_ref, 0), (j_ref, j_block_ref, h_slots)):
            for q in range(tiles.shape[1]):
                word = spot[s, first + q]
                strip = lax.shift_right_logical(word, bits)
                block[s, word & ((1 << bits) - 1), strip] = tiles[s, q].T


def turned(where, h_tiles, j_tiles, layout):
    column_tiles, row_tiles = layout[:2]
    sectors, _, tile, _ = h_tiles.shape
    vmem = pl.BlockSpec(memory_space=pltpu.VMEM)
    shapes = [(sectors, column_tiles, row_tiles * n + 1, tile, tile) for n in (1, J_OPERATORS)]
    moved_bytes = 4 * (h_tiles.size + j_tiles.size)
    return pl.pallas_call(
        functools.partial(turn_kernel, layout),
        out_shape=[jax.ShapeDtypeStruct(shape, h_tiles.dtype) for shape in shapes],
        in_specs=[pl.BlockSpec(memory_space=pl.ANY), vmem, vmem],
        out_specs=[vmem, vmem],
        scratch_shapes=[pltpu.SMEM(where.shape, jnp.int32), pltpu.SemaphoreType.DMA],
        compiler_params=pltpu.CompilerParams(vmem_limit_bytes=4 << 20),
        cost_estimate=pl.CostEstimate(flops=0, transcendentals=0, bytes_accessed=moved_bytes),
        name="turned",
    )(where, h_tiles, j_tiles)


def product_kernel(layout, half, *refs):
    column_tiles, row_tiles, group, halves, stride, pieces, bits = layout
    vector_refs, (h_block_ref, j_block_ref, out_ref) = refs[:pieces], refs[pieces:]
    kept_tiles, operators = row_tiles // halves, J_OPERATORS + 1
    tile = h_block_ref.shape[-1]
    each = column_tiles // pieces
    for s in range(out_ref.shape[0]):
        lined = jnp.concatenate(
            [vector_ref[s, :, t * tile : (t + 1) * tile] for vector_ref in vector_refs for t in range(each)], 1
        )
        for block_ref, first, count in ((j_block_ref, 1, J_OPERATORS), (h_block_ref, 0, 1)):
            start, stop = half * kept_tiles * count, (half + 1) * kept_tiles * count
            for strip in range(start, stop, 4):
                strips = range(strip, min(strip + 4, stop))
                block = [jnp.concatenate([block_ref[s, c, n] for n in strips], 1) for c in range(column_tiles)]
                product = jnp.dot(lined, jnp.concatenate(block, 0), preferred_element_type=jnp.float32)
                for i, n in enumerate(strips):
                    at = n // count % kept_tiles * operators + first + n % count
                    out_ref[s, at] = product[:, i * tile : (i + 1) * tile]


def tile_products(vectors, h_block, j_block, layout, half):
    column_tiles, row_tiles, group, halves, stride, pieces, bits = layout
    sectors, count_vectors = vectors[0].shape[:2]
    tile = h_block.shape[-1]
    count = row_tiles // halves * (J_OPERATORS + 1)
    vmem = pl.BlockSpec(memory_space=pltpu.VMEM)
    return pl.pallas_call(
        functools.partial(product_kernel, layout, half),
        out_shape=jax.ShapeDtypeStruct((sectors, count, count_vectors, tile), jnp.float32),
        in_specs=[vmem] * (pieces + 2),
        out_specs=vmem,
        compiler_params=pltpu.CompilerParams(vmem_limit_bytes=4 << 20),
        cost_estimate=pl.CostEstimate(
            flops=2 * sectors * count * count_vectors * tile * tile * column_tiles,
            transcendentals=0,
            bytes_accessed=2 * sectors * count * tile * tile * column_tiles,
        ),
        name="tile_products",
    )(*vectors, h_block, j_block)


def gram_kernel(x_ref, out_ref):
    sectors, count, vectors, _ = x_ref.shape
    operators = J_OPERATORS + 1
    out_ref[...] = jnp.zeros_like(out_ref)
    for s in range(sectors):
        strips = [x_ref[s, t * operators : (t + 1) * operators] for t in range(count // operators)]
        right = jnp.concatenate([strip.reshape(operators * vectors, -1) for strip in strips], 1)
        out_ref[s, :, : operators * vectors] = lax.dot_general(
            right[:vectors],
            right,
            (((1,), (1,)), ((), ())),
            precision=exact_precision,
            preferred_element_type=jnp.float32,
        )


def gram_parts(x):
    sectors, _, vectors, _ = x.shape
    vmem = pl.BlockSpec(memory_space=pltpu.VMEM)
    return pl.pallas_call(
        gram_kernel,
        out_shape=jax.ShapeDtypeStruct((sectors, vectors, LANES), jnp.float32),
        in_specs=[vmem],
        out_specs=vmem,
        compiler_params=pltpu.CompilerParams(vmem_limit_bytes=4 << 20),
        name="gram_parts",
    )(x)


def columns_of(matrix, first, count, width):
    return [jnp.broadcast_to(matrix[:, k : k + 1], (count, width)) for k in range(first, first + count)]


def product_of(columns, right):
    parts = [column * right[k : k + 1, :] for k, column in enumerate(columns)]
    while len(parts) > 1:
        parts = [functools.reduce(jnp.add, parts[i : i + 2]) for i in range(0, len(parts), 2)]
    return parts[0]


def root_kernel(layout, gram_ref, x_ref, basis_ref, elements_ref):
    total_rows, own_tiles, piece, group, halves = layout
    first = lax.axis_index("col") * piece // x_ref.shape[-1]
    own = first if halves == 1 else first // (group * halves) * group + first % group
    vectors, tile = x_ref.shape[2:]
    operators = J_OPERATORS + 1
    shape = (vectors, LANES)
    lanes = lax.broadcasted_iota(jnp.int32, shape, 1)
    is_gram = lanes < vectors
    ranks = lax.broadcasted_iota(jnp.int32, (vectors, 1), 0)
    steps = [jnp.where(ranks == k, 1.5, 0.0).astype(jnp.float32) for k in range(vectors)]
    for s in range(x_ref.shape[0]):
        held = gram_ref[s]
        columns = columns_of(held, 0, vectors, LANES)
        squares = jnp.where(is_gram, held * held, 0.0)
        squares = jnp.sum(jnp.sum(squares, axis=0, keepdims=True), axis=1, keepdims=True)
        scale = jnp.sqrt(squares + 1e-06)
        held = jnp.where(is_gram, held / scale, held)
        blocks = [x_ref[s, (own + t) * operators] for t in range(own_tiles)]
        half = 0.5 / scale
        for iteration in range(NSIT):
            middle = [step - half * column for step, column in zip(steps, columns)]
            once = product_of(middle, held)
            blocks = [product_of(middle, block) for block in blocks]
            if iteration < NSIT - 1:
                held = jnp.where(is_gram, product_of(middle, once), once)
                columns, half = columns_of(held, 0, vectors, LANES), 0.5
            else:
                held = once
        factor = jnp.sqrt(total_rows / scale)
        for t, block in enumerate(blocks):
            basis_ref[s, :, t * tile : (t + 1) * tile] = block * factor
        held = held * (factor / math.sqrt(total_rows))
        for a in range(J_OPERATORS):
            elements_ref[s, a] = held[:, (a + 1) * vectors : (a + 2) * vectors]


def orthonormal(gram, x, layout):
    sectors, _, vectors, tile = x.shape
    vmem = pl.BlockSpec(memory_space=pltpu.VMEM)
    return pl.pallas_call(
        functools.partial(root_kernel, layout),
        out_shape=[
            jax.ShapeDtypeStruct((sectors, vectors, layout[1] * tile), jnp.float32),
            jax.ShapeDtypeStruct((sectors, J_OPERATORS, vectors, vectors), jnp.float32),
        ],
        in_specs=[vmem, vmem],
        out_specs=[vmem, vmem],
        compiler_params=pltpu.CompilerParams(vmem_limit_bytes=4 << 20),
        name="orthonormal",
    )(gram, x)


def per_device(vectors, h_tiles, h_list, j_tiles, j_list):
    sectors, _, piece = vectors.shape
    tile = h_tiles.shape[-1]
    n_row, n_col = lax.axis_size("row"), lax.axis_size("col")
    column = lax.axis_index("col")
    block_rows = piece * n_col
    row_tiles = block_rows // tile
    column_tiles = piece * n_row // tile
    total_rows = block_rows * n_row
    digit = scatter_digit(n_col, piece, tile)
    halves = 1 if digit is None else 2
    group = 1 if digit is None else piece * digit[0] // tile
    stride = 1 if digit is None else digit[0]
    direct = piece == tile and n_row in (2, 4)

    if direct:
        parts = [vectors]
        for mask in range(1, n_row):
            parts.append(lax.ppermute(vectors, "row", [(i, i ^ mask) for i in range(n_row)]))
    else:
        parts = [lax.all_gather(vectors, "row", axis=2, tiled=True)]
    bits = (column_tiles - 1).bit_length()
    layout = (column_tiles, row_tiles, group, halves, stride, len(parts), bits)
    where = spots(h_list.reshape(sectors, -1), j_list.reshape(sectors, -1), layout)
    h_block, j_block = turned(
        where, h_tiles.reshape(sectors, -1, tile, tile), j_tiles.reshape(sectors, -1, tile, tile), layout
    )
    arriving = None
    if digit is not None:
        arriving = sent(tile_products(parts, h_block, j_block, layout, 1), "col", digit, 1)
    x = tile_products(parts, h_block, j_block, layout, 0)
    if digit is not None:
        x = x + arriving
    for other in digits_of(n_col):
        if other != digit:
            x = summed(x, "col", other)

    gram = gram_parts(x)
    if direct and n_row == 4 and digit is not None:
        gram = gram + across(gram, 1, 0) + across(gram, 2, 0) + across(gram, 3, 0)
        gram = gram + across(gram, 0, digit[0])
    else:
        for other in digits_of(n_row):
            gram = summed(gram, "row", other)
        if digit is not None:
            gram = summed(gram, "col", digit)

    own_tiles = max(1, piece // tile)
    basis, elements = orthonormal(gram, x, (total_rows, own_tiles, piece, group, halves))
    if piece < tile:
        basis = lax.dynamic_slice_in_dim(basis, column * piece % tile, piece, 2)
    return (basis, elements)


def solution(mesh):
    return jax.shard_map(
        per_device,
        mesh=mesh,
        in_specs=(
            P(None, None, ("col", "row")),
            P(None, "row", "col", None, None),
            P(None, "row", "col"),
            P(None, "row", "col", None, None),
            P(None, "row", "col"),
        ),
        out_specs=(P(None, None, ("row", "col")), P()),
        check_vma=False,
    )
```
